256 devices in a mesh: row: 16 (over y, z_lo), col: 16 (over x, z_hi, core).
Axes of the slice: x: 4, y: 4, z: 8 (z_hi: 2, z_lo: 4; z = z_hi * 4 + z_lo), core: 2. Of those that a mesh axis runs over, the one named last changes fastest.
Arguments:
- object_tiles: float32 [4, 4096, 4096], P(None, 'row', 'col'), may hold values from -6 to 6
- probe: float32 [2, 128, 128], replicated, may hold values from -6 to 6
- prop_phase: float32 [128, 128], replicated, may hold values from -3.140625 to 3.140625
- amplitudes: float32 [4, 2048, 2048], P(None, 'row', 'col'), may hold values from 0.5 to 3
- offsets: int32 [16, 16, 4, 2], P('row', 'col'), may hold values from -64 to 191, as said below
- counts: int32 [16, 16], P('row', 'col'), may hold values from 1 to 4, as said below
Outputs:
- updated_object: float32 [4, 4096, 4096], P(None, 'row', 'col')
The draws below stay inside these ranges and needn't reach their ends.
Inputs may be any that keep to these rules, and one draw needn't show every extreme that they name: Only the first counts[r, c] slots of a tile are used. Slot 0 of some tile has both offsets at the least value, slot 0 of another tile both at the greatest. `counts`: most tiles use one probe; some tile uses 4 and some other tile uses one.
All inputs are finite; a program needn't handle non-finite values.
Results may differ from the reference program's by a relative error of at most 0.025.
Values sent between devices are 32-bit elements; how exact they have to be, the bound alone decides.
No kernel may reach another device: no remote copies, remote signals or barrier semaphores. Data moves between devices by JAX's collectives and lax.ppermute only.
A program may use at most 64 MiB of HBM per device.

```python
import math
import jax
import jax.numpy as jnp
from jax import lax

S = 128
TILE = 256
PROBE_SLOTS = 4
LAYERS = 2
ITERS = 2
HALF = 64
OBJ_ROWS = 4096
OBJ_COLS = 4096
MEASURED_ROWS = 2048
MEASURED_COLUMNS = 2048
N_ROW = 16
N_COL = 16


def draw_offsets(key, part):
    lowest = -HALF
    highest = TILE - HALF - 1
    tile_total = N_ROW * N_COL
    flat_values = jax.random.randint(jax.random.fold_in(key, 11), (tile_total, PROBE_SLOTS, 2), lowest, highest + 1, dtype=jnp.int32)
    first_pick = jax.random.randint(jax.random.fold_in(key, 12), (), 0, tile_total, dtype=jnp.int32)
    later_selection = (first_pick + 1 + jax.random.randint(jax.random.fold_in(key, 13), (), 0, tile_total - 1, dtype=jnp.int32)) % tile_total
    tile_ids = jnp.arange(tile_total, dtype=jnp.int32)[:, None, None]
    slot_ids = jnp.arange(PROBE_SLOTS, dtype=jnp.int32)[None, :, None]
    flat_values = jnp.where((tile_ids == first_pick) & (slot_ids == 0), lowest, flat_values)
    flat_values = jnp.where((tile_ids == later_selection) & (slot_ids == 0), highest, flat_values)
    return flat_values.reshape(N_ROW, N_COL, PROBE_SLOTS, 2).astype(jnp.int32)


def draw_counts(key, part):
    tile_total = N_ROW * N_COL
    extra_count = jax.random.randint(jax.random.fold_in(key, 21), (tile_total,), 1, PROBE_SLOTS, dtype=jnp.int32)
    raised_power = jax.random.randint(jax.random.fold_in(key, 22), (tile_total,), 0, 8, dtype=jnp.int32) >= 5
    flat_values = 1 + jnp.where(raised_power, extra_count, 0)
    chosen = jax.random.randint(jax.random.fold_in(key, 23), (), 0, tile_total, dtype=jnp.int32)
    tile_ids = jnp.arange(tile_total, dtype=jnp.int32)
    flat_values = jnp.where(tile_ids == chosen, PROBE_SLOTS, flat_values)
    flat_values = jnp.where(tile_ids == (chosen + 1) % tile_total, 1, flat_values)
    return flat_values.reshape(N_ROW, N_COL).astype(jnp.int32)


def block_scale(own_key, shape, split, low, high):
    level, own = 1.0, jax.random.fold_in(own_key, 6)
    for position, blocks in split:
        heights = jnp.exp(jax.random.uniform(jax.random.fold_in(own, position), (blocks,), jnp.float32, low / len(split), high / len(split)))
        level = level * jnp.repeat(heights, shape[position] // blocks).reshape([-1 if axis == position else 1 for axis in range(len(shape))])
    return level


def normal_values(key, dims, spread, reach, split=(), kind=jnp.bfloat16):
    values = spread * jax.random.normal(key, dims, jnp.float32)
    if split:
        values = values * block_scale(key, dims, split, -0.22, 0.18)
    return jnp.clip(values, -reach, reach).astype(kind)


def setup_inputs(seed: int = 0) -> dict:
    splits = jax.random.split(jax.random.key(seed), 7)
    object_tiles = normal_values(splits[0], (2 * LAYERS, OBJ_ROWS, OBJ_COLS), 1.0, 6.0, ((1, 16), (2, 16)), jnp.float32)
    probe = normal_values(splits[1], (2, S, S), 1.0, 6.0, (), jnp.float32)
    prop_phase = jnp.clip(jax.random.uniform(splits[2], (S, S), jnp.float32, -3.140625, 3.140625), -3.140625, 3.140625)
    amplitudes = jnp.clip(0.5 + 2.5 * jax.random.uniform(splits[3], (PROBE_SLOTS, MEASURED_ROWS, MEASURED_COLUMNS), jnp.float32) ** block_scale(splits[3], (PROBE_SLOTS, MEASURED_ROWS, MEASURED_COLUMNS), ((1, 16), (2, 16)), -0.2, 0.2), 0.5, 3.0)
    offsets = draw_offsets(jax.random.fold_in(splits[6], 71), 0)
    counts = draw_counts(jax.random.fold_in(splits[6], 71), 0)
    return dict(object_tiles=object_tiles, probe=probe, prop_phase=prop_phase, amplitudes=amplitudes, offsets=offsets, counts=counts)


def fourier_tables(size, direction_sign):
    indices = jnp.arange(size, dtype=jnp.int32)
    products = indices[:, None] * indices[None, :] % size
    phases = products.astype(jnp.float32) * (2.0 * math.pi / size)
    norm_scale = 1.0 / math.sqrt(size)
    cosine = jnp.cos(phases) * norm_scale
    sine_part = direction_sign * jnp.sin(phases) * norm_scale
    left_table = jnp.concatenate([jnp.concatenate([cosine, -sine_part], 1), jnp.concatenate([sine_part, cosine], 1)], 0)
    right_table = jnp.concatenate([jnp.concatenate([cosine, sine_part], 1), jnp.concatenate([-sine_part, cosine], 1)], 0)
    return (left_table.astype(jnp.bfloat16), right_table.astype(jnp.bfloat16))

def transform(values, tables):
    size = values[0].shape[-1]
    stacked = lax.optimization_barrier(jnp.concatenate([values[0], values[1]], axis=1).astype(jnp.bfloat16)).astype(jnp.float32)
    half_done = jnp.einsum('ij,bjk->bik', tables[0].astype(jnp.float32), stacked, precision=lax.Precision.HIGHEST)
    half_done = lax.optimization_barrier(half_done.astype(jnp.bfloat16)).astype(jnp.float32)
    sided = jnp.concatenate([half_done[:, :size], half_done[:, size:]], axis=2)
    sweep_result = jnp.einsum('bij,jk->bik', sided, tables[1].astype(jnp.float32), precision=lax.Precision.HIGHEST)
    return (sweep_result[..., :size], sweep_result[..., size:])

def complex_times(first, second):
    return (first[0] * second[0] - first[1] * second[1], first[0] * second[1] + first[1] * second[0])

def conjugate(values):
    return (values[0], -values[1])

def probe_terms(windows, measured, probe_wave, propagator, forward_tables, inverse_tables):
    object_one = (windows[:, 0], windows[:, 1])
    object_two = (windows[:, 2], windows[:, 3])
    first_exit = complex_times(probe_wave, object_one)
    spectrum = transform(first_exit, forward_tables)
    inner_wave = transform(complex_times(propagator, spectrum), inverse_tables)
    far_field = transform(complex_times(inner_wave, object_two), forward_tables)
    magnitude = jnp.sqrt(far_field[0] * far_field[0] + far_field[1] * far_field[1])
    keep_part = 1.0 - measured / jnp.maximum(magnitude, 1.0)
    back_far = transform((far_field[0] * keep_part, far_field[1] * keep_part), inverse_tables)
    gradient_later_slice = complex_times(conjugate(inner_wave), back_far)
    illum_second = inner_wave[0] * inner_wave[0] + inner_wave[1] * inner_wave[1]
    back_inner = complex_times(conjugate(object_two), back_far)
    back_spec = complex_times(conjugate(propagator), transform(back_inner, forward_tables))
    back_first = transform(back_spec, inverse_tables)
    grad_first = complex_times(conjugate(probe_wave), back_first)
    illum_first = jnp.broadcast_to(probe_wave[0] * probe_wave[0] + probe_wave[1] * probe_wave[1], magnitude.shape)
    return jnp.stack([grad_first[0], grad_first[1], gradient_later_slice[0], gradient_later_slice[1], illum_first, illum_second], axis=1)

def reference(object_tiles, probe, prop_phase, amplitudes, offsets, counts):
    probe_wave = (probe[0], probe[1])
    propagator = (jnp.cos(prop_phase), jnp.sin(prop_phase))
    forward_tables = fourier_tables(S, -1.0)
    inverse_tables = fourier_tables(S, 1.0)
    total_rows = TILE * N_ROW
    total_cols = TILE * N_COL
    current = object_tiles
    for sweep in range(ITERS):
        padded = jnp.pad(current, ((0, 0), (HALF, HALF), (HALF, HALF)))

        def add_probe(flat_index, gradients):
            flat_index = flat_index.astype(jnp.int32)
            tile_row = (flat_index // (N_COL * PROBE_SLOTS)).astype(jnp.int32)
            tile_col = (flat_index // PROBE_SLOTS % N_COL).astype(jnp.int32)
            slot = (flat_index % PROBE_SLOTS).astype(jnp.int32)
            row_start = (tile_row * TILE + offsets[tile_row, tile_col, slot, 0] + HALF).astype(jnp.int32)
            col_start = (tile_col * TILE + offsets[tile_row, tile_col, slot, 1] + HALF).astype(jnp.int32)
            zero_index = jnp.zeros((), jnp.int32)
            start = (zero_index, row_start, col_start)

            def compute(grads_in):
                window = lax.dynamic_slice(padded, start, (4, S, S))
                measured = lax.dynamic_slice(amplitudes, (slot, (tile_row * S).astype(jnp.int32), (tile_col * S).astype(jnp.int32)), (1, S, S))
                contribution = probe_terms(window[None], measured, probe_wave, propagator, forward_tables, inverse_tables)[0]
                existing = lax.dynamic_slice(grads_in, start, (6, S, S))
                return lax.dynamic_update_slice(grads_in, existing + contribution, start)

            def keep_same(grads_in):
                return grads_in
            return lax.cond(slot < counts[tile_row, tile_col], compute, keep_same, gradients)
        gradients = lax.fori_loop(0, N_ROW * N_COL * PROBE_SLOTS, add_probe, jnp.zeros((6, total_rows + 2 * HALF, total_cols + 2 * HALF), jnp.float32))
        summed = gradients[:, HALF:HALF + total_rows, HALF:HALF + total_cols]
        divisor = jnp.repeat(summed[4:6], 2, axis=0) + 1.0
        current = current - summed[:4] / divisor
    return current
```

```python
import jax
import jax.numpy as jnp
import numpy as np
from jax import lax
from jax.experimental import pallas as pl
from jax.experimental.pallas import tpu as pltpu
from jax.sharding import PartitionSpec as P

S = 128
HALF = 64
TILE = 256
SLOTS = 4
LONG = S + 8
FAR = 1 << 20
COLS = 520
ROWS = 776
LIMIT = 56 * 1024 * 1024
F32 = jnp.float32
I32 = jnp.int32

NEAR_PAIRS = [(i, i ^ 1) for i in range(16)]
FAR_PAIRS = [(i, ((i + 1) ^ 1) - 1) for i in range(1, 15)]
COL_SIZES = (0, 1, 2, 3, 4)
ROW_SIZES = (0, 1, 2, 3, 4, 5, 6, 8, 12)

T_SEND = 0
T_N0 = 4
T_N1 = 5
T_NV = 6
T_ROW = 8
T_RELAY = 16
T_LIST1 = 80
T_MAIN = 128
T_SIZE = 384


def wave_tables():
    index = np.arange(S)
    phase = (index[:, None] * index[None, :] % S) * (2.0 * np.pi / S)
    cosine = np.cos(phase) / np.sqrt(S)
    sine = np.sin(phase) / np.sqrt(S)
    first = np.block([[cosine, sine], [-sine, cosine]])
    second = np.block([[cosine, -sine], [sine, cosine]])
    return np.stack([first, second]).astype(jnp.bfloat16)


def roll(x, by):
    return pltpu.roll(x, by, 1)


def pack_cols(info, tile, near, far):
    lane = lax.broadcasted_iota(I32, (TILE, 128), 1)
    low = lane < HALF
    odd = (lane * 0 + info[9]) == 1
    for q in range(2):
        a0, a1 = tile[2 * q, :, 0:128], tile[2 * q, :, 128:256]
        b0, b1 = tile[2 * q + 1, :, 0:128], tile[2 * q + 1, :, 128:256]
        left = jnp.where(low, a0, roll(b0, HALF))
        right = jnp.where(low, roll(a1, HALF), b1)
        rows = slice(q * TILE, (q + 1) * TILE)
        near[rows, :] = jnp.where(odd, left, right)
        far[rows, :] = jnp.where(odd, right, left)
    lane = lax.broadcasted_iota(I32, (8, 128), 1)
    meta = jnp.zeros((8, 128), I32)
    for k in range(9):
        meta = jnp.where(lane == k, info[k], meta)
    meta = meta.astype(F32)
    near[512:520, :] = meta
    far[512:520, :] = meta


def pack_rows(info, tile, near, far, wide, out_near, out_far):
    lane = lax.broadcasted_iota(I32, (TILE, 128), 1)
    low = lane < HALF
    odd = (lane * 0 + info[9]) == 1
    odd_row = ((lane * 0 + info[10]) == 1)[:HALF]
    for q in range(2):
        rows = slice(q * TILE, (q + 1) * TILE)
        left = jnp.where(odd, near[rows, :], far[rows, :])
        right = jnp.where(odd, far[rows, :], near[rows, :])
        for k in range(2):
            p = 2 * q + k
            t0, t1 = roll(tile[p, :, 0:128], HALF), roll(tile[p, :, 128:256], HALF)
            lft = left if k == 0 else roll(left, HALF)
            rgt = roll(right, HALF) if k == 0 else right
            parts = (jnp.where(low, lft, t0), jnp.where(low, t0, t1), jnp.where(low, t1, rgt))
            for b in range(3):
                wide[p, :, b * 128 : (b + 1) * 128] = parts[b]
                top, bottom = parts[b][:HALF], parts[b][TILE - HALF :]
                at = slice((p * 3 + b) * HALF, (p * 3 + b + 1) * HALF)
                out_near[at, :] = jnp.where(odd_row, top, bottom)
                out_far[at, :] = jnp.where(odd_row, bottom, top)
    lane = lax.broadcasted_iota(I32, (8, 128), 1)
    row = lax.broadcasted_iota(I32, (8, 128), 0)
    odd = (lane * 0 + info[9]) == 1
    mine = jnp.zeros((8, 128), I32)
    for k in range(9):
        mine = jnp.where(lane == k, info[k], mine)
    left = jnp.where(odd, near[512:520, :], far[512:520, :])
    right = jnp.where(odd, far[512:520, :], near[512:520, :])
    meta = jnp.where(row == 0, left, jnp.where(row == 1, mine.astype(F32), right))
    out_near[768:776, :] = meta
    out_far[768:776, :] = meta


def tile_touch(r, c, row0, col0):
    return (r < row0 + TILE) & (r + S > row0) & (c < col0 + TILE) & (c + S > col0)


def pick(ref, lead, r, c, lane):
    line = pl.multiple_of((r // 8) * 8, 8)
    block = pl.multiple_of((c // 128) * 128, 128)
    rest = c % 128
    back = (128 - rest) % 128
    up = (LONG - r % 8) % LONG
    one = roll(ref[lead, pl.ds(line, LONG), pl.ds(block, 128)], back)
    two = roll(ref[lead, pl.ds(line, LONG), pl.ds(block + 128, 128)], back)
    return pltpu.roll(jnp.where(lane < 128 - rest, one, two), up, 0)[:S]


def put(ref, lead, r, c, value, lane):
    line = pl.multiple_of((r // 8) * 8, 8)
    block = pl.multiple_of((c // 128) * 128, 128)
    rest = c % 128
    moved = jnp.concatenate([value, jnp.zeros((8, 128), F32)], axis=0)
    moved = roll(pltpu.roll(moved, r % 8, 0), rest)
    zero = jnp.zeros_like(moved)
    ref[lead, pl.ds(line, LONG), pl.ds(block, 128)] += jnp.where(lane >= rest, moved, zero)
    ref[lead, pl.ds(line, LONG), pl.ds(block + 128, 128)] += jnp.where(lane < rest, moved, zero)


def make_records(
    info, wide, v_near, v_far, meta_near, meta_far, amps, own, s_near, s_far, tbl, ext, vec, meta_s, need_s, sems
):
    lane8 = lax.broadcasted_iota(I32, (8, 128), 1)
    row8 = lax.broadcasted_iota(I32, (8, 128), 0)
    odd_row = (lane8 * 0 + info[10]) == 1
    odd = (lane8 * 0 + info[9]) == 1
    up = jnp.where(odd_row, v_near[768:776, :], v_far[768:776, :])
    down = jnp.where(odd_row, v_far[768:776, :], v_near[768:776, :])
    mine = jnp.zeros((8, 128), I32)
    for k in range(9):
        mine = jnp.where(lane8 == k, info[k], mine)
    left = jnp.where(odd, meta_near[...], meta_far[...])
    right = jnp.where(odd, meta_far[...], meta_near[...])
    middle = jnp.where(row8 == 0, left, jnp.where(row8 == 1, mine.astype(F32), right))
    vec[0:8, :] = up.astype(I32)
    vec[8:16, :] = middle.astype(I32)
    vec[16:24, :] = down.astype(I32)
    copy = pltpu.make_async_copy(vec, meta_s, sems.at[0])
    copy.start()

    half_odd = (lax.broadcasted_iota(I32, (HALF, 128), 1) * 0 + info[10]) == 1
    for p in range(4):
        ext[p, HALF : HALF + TILE, :] = wide[p]
        for b in range(3):
            at = slice((p * 3 + b) * HALF, (p * 3 + b + 1) * HALF)
            cols = slice(b * 128, (b + 1) * 128)
            one, two = v_near[at, :], v_far[at, :]
            ext[p, 0:HALF, cols] = jnp.where(half_odd, one, two)
            ext[p, HALF + TILE :, cols] = jnp.where(half_odd, two, one)
    copy.wait()

    lane = lax.broadcasted_iota(I32, (16, 128), 1)
    tile_row = lax.broadcasted_iota(I32, (16, 128), 0)
    row0 = (tile_row // 3 - 1) * TILE
    col0 = (tile_row % 3 - 1) * TILE
    rows_v = jnp.full((16, 128), FAR, I32)
    cols_v = jnp.full((16, 128), FAR, I32)
    where_r, where_c = [], []
    for j in range(36):
        t, s = j // SLOTS, j % SLOTS
        at = (t // 3) * 8 + t % 3
        used = s < meta_s[at, 0]
        r = jnp.where(used, meta_s[at, 1 + 2 * s] + (t // 3 - 1) * TILE, FAR)
        c = jnp.where(used, meta_s[at, 2 + 2 * s] + (t % 3 - 1) * TILE, FAR)
        where_r.append(r)
        where_c.append(c)
        rows_v = jnp.where(lane == j, r, rows_v)
        cols_v = jnp.where(lane == j, c, cols_v)
    need = tile_touch(rows_v, cols_v, row0, col0)
    for j in range(36):
        r, c = where_r[j], where_c[j]
        over = (rows_v - r < S) & (r - rows_v < S) & (cols_v - c < S) & (c - cols_v < S)
        need = need | (tile_touch(r, c, row0, col0) & over)
    there_row = tile_row // 3 - 1 + info[11]
    there_col = tile_row % 3 - 1 + info[12]
    inside = (there_row >= 0) & (there_row < 16) & (there_col >= 0) & (there_col < 16)
    used = rows_v < FAR
    vec[0:16, :] = jnp.where(need & inside & used, 1, 0)
    copy = pltpu.make_async_copy(vec.at[0:16], need_s, sems.at[0])
    copy.start()
    lane_s = lax.broadcasted_iota(I32, (LONG, S), 1)
    for s in range(SLOTS):

        @pl.when(s < info[0])
        def _():
            r = info[1 + 2 * s] + HALF
            c = info[2 + 2 * s] + HALF
            for p in range(4):
                own[s, p] = pick(ext, p, r, c, lane_s)
            own[s, 4] = amps[s]

    copy.wait()

    side_near = 1 - 2 * info[9]
    row_near = 1 - 2 * info[10]
    tbl[T_N0] = 0
    tbl[T_N1] = 0
    tbl[T_NV] = 0
    tbl[T_NV + 1] = 0
    tbl[T_ROW] = info[11] * TILE
    tbl[T_ROW + 1] = info[12] * TILE

    def add_main(buf, pos, r, c):
        n0 = tbl[T_N0]
        tbl[T_MAIN + 4 * n0] = buf
        tbl[T_MAIN + 4 * n0 + 1] = pos
        tbl[T_MAIN + 4 * n0 + 2] = r
        tbl[T_MAIN + 4 * n0 + 3] = c
        tbl[T_N0] = n0 + 1

        @pl.when(tile_touch(r, c, 0, 0))
        def _():
            n1 = tbl[T_N1]
            tbl[T_LIST1 + n1] = n0
            tbl[T_N1] = n1 + 1

    def add_relay(j, buf, pos):
        for e, side in enumerate((row_near, -row_near)):

            @pl.when(need_s[(side + 1) * 3 + 1, j] == 1)
            def _():
                n = tbl[T_NV + e]
                tbl[T_RELAY + 24 * e + 2 * n] = buf
                tbl[T_RELAY + 24 * e + 2 * n + 1] = pos
                tbl[T_NV + e] = n + 1

    def place(j):
        t, s = j // SLOTS, j % SLOTS
        at = (t // 3) * 8 + t % 3
        return (
            meta_s[at, 1 + 2 * s] + (t // 3 - 1) * TILE,
            meta_s[at, 2 + 2 * s] + (t % 3 - 1) * TILE,
        )

    sent = []
    for side, buf in ((side_near, s_near), (-side_near, s_far)):
        count = jnp.int32(0)
        for s in range(SLOTS):
            j = 16 + s
            flag = need_s[side + 1, j] | need_s[side + 4, j] | need_s[side + 7, j]

            @pl.when(flag == 1)
            def _():
                buf[count] = own[s]

            count = count + flag
        sent.append(count)
    for s in range(SLOTS):

        @pl.when(s < info[0])
        def _():
            add_main(0, s, info[1 + 2 * s], info[2 + 2 * s])
            add_relay(16 + s, 0, s)

    got = []
    for side in (-1, 1):
        buf = jnp.where(side_near == side, 1, 2)
        count = jnp.int32(0)
        for s in range(SLOTS):
            j = (4 + side) * SLOTS + s
            flag = need_s[1, j] | need_s[4, j] | need_s[7, j]

            @pl.when(flag == 1)
            def _():
                @pl.when(need_s[4, j] == 1)
                def _():
                    r, c = place(j)
                    add_main(buf, count, r, c)

                add_relay(j, buf, count)

            count = count + flag
        got.append(count)
    got_near = jnp.where(side_near == 1, got[1], got[0])
    got_far = jnp.where(side_near == 1, got[0], got[1])
    tbl[T_SEND] = jnp.maximum(sent[0], got_near)
    tbl[T_SEND + 1] = jnp.maximum(sent[1], got_far)

    got = []
    for side in (-1, 1):
        buf = jnp.where(row_near == side, 3, 4)
        count = jnp.int32(0)
        for t in (4 + 3 * side, 3 + 3 * side, 5 + 3 * side):
            for s in range(SLOTS):
                j = t * SLOTS + s
                flag = need_s[4, j]

                @pl.when(flag == 1)
                def _():
                    r, c = place(j)
                    add_main(buf, count, r, c)

                count = count + flag
        got.append(count)
    got_near = jnp.where(row_near == 1, got[1], got[0])
    got_far = jnp.where(row_near == 1, got[0], got[1])
    for e, arrived in enumerate((got_near, got_far)):
        most = jnp.maximum(tbl[T_NV + e], arrived)
        tbl[T_SEND + 2 + e] = jnp.where(most <= 6, most, jnp.where(most <= 8, 7, 8))


def relay(tbl, own, h_near, h_far, v_near, v_far, stage, in_sem, out_sem):
    for e, target in enumerate((v_near, v_far)):

        @pl.loop(0, tbl[T_NV + e])
        def _(i):
            buf = tbl[T_RELAY + 24 * e + 2 * i]
            pos = tbl[T_RELAY + 24 * e + 2 * i + 1]
            for b, source in enumerate((own, h_near, h_far)):

                @pl.when(buf == b)
                def _():
                    pltpu.make_async_copy(source.at[pos], stage.at[12 * e + i], in_sem.at[12 * e + i]).start()

    for e, target in enumerate((v_near, v_far)):

        @pl.loop(0, tbl[T_NV + e])
        def _(i):
            pltpu.make_async_copy(own.at[0], stage.at[12 * e + i], in_sem.at[12 * e + i]).wait()
            pltpu.make_async_copy(stage.at[12 * e + i], target.at[i], out_sem.at[12 * e + i]).start()

    for e, target in enumerate((v_near, v_far)):

        @pl.loop(0, tbl[T_NV + e])
        def _(i):
            pltpu.make_async_copy(stage.at[12 * e + i], target.at[i], out_sem.at[12 * e + i]).wait()


def times(a, b):
    return (a[0] * b[0] - a[1] * b[1], a[0] * b[1] + a[1] * b[0])


def conj_times(a, b):
    return (a[0] * b[0] + a[1] * b[1], a[0] * b[1] - a[1] * b[0])


def transform(x, left, right):
    half = jnp.concatenate([x[0].astype(jnp.bfloat16), x[1].astype(jnp.bfloat16)], axis=0)
    half = jnp.dot(left, half, preferred_element_type=F32).astype(jnp.bfloat16)
    half = jnp.concatenate([half[:S], half[S:]], axis=1)
    done = jnp.dot(half, right, preferred_element_type=F32)
    return (done[:, :S], done[:, S:])


def sweeps(tbl, tile, probe, prop, waves, own, h_near, h_far, v_near, v_far, out, rec, acc, sems):
    n0 = tbl[T_N0]
    n1 = tbl[T_N1]

    @pl.loop(0, n0)
    def _(i):
        buf = tbl[T_MAIN + 4 * i]
        pos = tbl[T_MAIN + 4 * i + 1]
        for b, source in enumerate((own, h_near, h_far, v_near, v_far)):

            @pl.when(buf == b)
            def _():
                pltpu.make_async_copy(source.at[pos], rec.at[i], sems.at[i]).start()

    @pl.loop(0, 12)
    def _(p):
        acc[p, 128:640, 128:640] = jnp.zeros((512, 512), F32)

    lane = lax.broadcasted_iota(I32, (LONG, S), 1)

    @pl.loop(0, n0 + n1)
    def _(i):
        second = i >= n0
        e = jnp.where(second, tbl[T_LIST1 + jnp.maximum(i - n0, 0)], i)
        r = tbl[T_MAIN + 4 * e + 2] + TILE
        c = tbl[T_MAIN + 4 * e + 3] + TILE
        base = jnp.where(second, 6, 0)

        @pl.when(jnp.logical_not(second))
        def _():
            pltpu.make_async_copy(own.at[0], rec.at[i], sems.at[i]).wait()

        @pl.when(second)
        def _():
            high = tbl[T_ROW] + r - TILE + lax.broadcasted_iota(I32, (S, S), 0)
            wide = tbl[T_ROW + 1] + c - TILE + lax.broadcasted_iota(I32, (S, S), 1)
            inside = (high >= 0) & (high < 16 * TILE) & (wide >= 0) & (wide < 16 * TILE)
            for k in range(2):
                scale = jnp.where(inside, 1.0 / (pick(acc, 4 + k, r, c, lane) + 1.0), 0.0)
                for p in (2 * k, 2 * k + 1):
                    rec[e, p] = rec[e, p] - pick(acc, p, r, c, lane) * scale

        wave = (probe[0], probe[1])
        spread = (prop[0], prop[1])
        one, two = waves[0], waves[1]
        exit_wave = times(wave, (rec[e, 0], rec[e, 1]))
        inner = transform(times(spread, transform(exit_wave, one, two)), two, one)
        o2 = (rec[e, 2], rec[e, 3])
        field = transform(times(inner, o2), one, two)
        size = jnp.sqrt(field[0] * field[0] + field[1] * field[1])
        keep = 1.0 - rec[e, 4] / jnp.maximum(size, 1.0)
        g2 = transform((field[0] * keep, field[1] * keep), two, one)
        later = conj_times(inner, g2)
        put(acc, base + 2, r, c, later[0], lane)
        put(acc, base + 3, r, c, later[1], lane)
        put(acc, base + 5, r, c, inner[0] * inner[0] + inner[1] * inner[1], lane)
        back = conj_times(spread, transform(conj_times(o2, g2), one, two))
        first = conj_times(wave, transform(back, two, one))
        put(acc, base, r, c, first[0], lane)
        put(acc, base + 1, r, c, first[1], lane)
        put(acc, base + 4, r, c, wave[0] * wave[0] + wave[1] * wave[1], lane)

    for k in range(2):
        one = 1.0 / (acc[4 + k, 256:512, 256:512] + 1.0)
        two = 1.0 / (acc[10 + k, 256:512, 256:512] + 1.0)
        for p in (2 * k, 2 * k + 1):
            out[p] = tile[p] - acc[p, 256:512, 256:512] * one - acc[6 + p, 256:512, 256:512] * two


VMEM = pl.BlockSpec(memory_space=pltpu.VMEM)
SMEM = pl.BlockSpec(memory_space=pltpu.SMEM)
ANY = pl.BlockSpec(memory_space=pl.ANY)
PARAMS = pltpu.CompilerParams(vmem_limit_bytes=LIMIT)


def shape(*dims, dtype=F32):
    return jax.ShapeDtypeStruct(dims, dtype)


def records(count):
    return shape(count, 5, S, S)


def nothing(out):
    pass


def exchange(sent, branch, axis, pairs, sizes):
    full = sent.shape

    def empty():
        return pl.pallas_call(nothing, out_shape=shape(*full), out_specs=ANY, name="blank")()

    def of(count):
        def run(value):
            if count == 0:
                return empty()
            got = lax.ppermute(value[:count], axis, pairs)
            if count == full[0]:
                return got
            return lax.dynamic_update_slice(empty(), got, (0, 0, 0, 0))

        return run

    return lax.switch(branch, [of(count) for count in sizes], sent)


def on_device(object_tiles, probe, prop_phase, amplitudes, offsets, counts):
    row = lax.axis_index("row").astype(I32)
    col = lax.axis_index("col").astype(I32)
    info = jnp.concatenate(
        [counts.reshape(1), offsets.reshape(8), jnp.stack([col % 2, row % 2, row, col]), jnp.zeros((3,), I32)]
    )
    near, far = pl.pallas_call(
        pack_cols,
        out_shape=(shape(COLS, 128), shape(COLS, 128)),
        in_specs=[SMEM, VMEM],
        out_specs=(VMEM, VMEM),
        compiler_params=PARAMS,
        name="pack_cols",
    )(info, object_tiles)
    far = lax.ppermute(far, "col", FAR_PAIRS)
    near = lax.ppermute(near, "col", NEAR_PAIRS)
    wide, near_v, far_v = pl.pallas_call(
        pack_rows,
        out_shape=(shape(4, TILE, 384), shape(ROWS, 128), shape(ROWS, 128)),
        in_specs=[SMEM, VMEM, VMEM, VMEM],
        out_specs=(VMEM, VMEM, VMEM),
        compiler_params=PARAMS,
        name="pack_rows",
    )(info, object_tiles, near, far)
    far_v = lax.ppermute(far_v, "row", FAR_PAIRS)
    near_v = lax.ppermute(near_v, "row", NEAR_PAIRS)
    own, s_near, s_far, tbl = pl.pallas_call(
        make_records,
        out_shape=(records(4), records(4), records(4), shape(T_SIZE, dtype=I32)),
        in_specs=[SMEM] + [VMEM] * 6,
        out_specs=(VMEM, VMEM, VMEM, SMEM),
        scratch_shapes=[
            pltpu.VMEM((4, 384, 384), F32),
            pltpu.VMEM((24, 128), I32),
            pltpu.SMEM((24, 128), I32),
            pltpu.SMEM((16, 128), I32),
            pltpu.SemaphoreType.DMA((1,)),
        ],
        compiler_params=PARAMS,
        name="make_records",
    )(info, wide, near_v, far_v, near[512:520], far[512:520], amplitudes)
    h_near = exchange(s_near, tbl[T_SEND], "col", NEAR_PAIRS, COL_SIZES)
    h_far = exchange(s_far, tbl[T_SEND + 1], "col", FAR_PAIRS, COL_SIZES)
    s_near, s_far = pl.pallas_call(
        relay,
        out_shape=(records(12), records(12)),
        in_specs=[SMEM, ANY, ANY, ANY],
        out_specs=(ANY, ANY),
        scratch_shapes=[
            pltpu.VMEM((24, 5, S, S), F32),
            pltpu.SemaphoreType.DMA((24,)),
            pltpu.SemaphoreType.DMA((24,)),
        ],
        compiler_params=PARAMS,
        name="relay",
    )(tbl, own, h_near, h_far)
    v_near = exchange(s_near, tbl[T_SEND + 2], "row", NEAR_PAIRS, ROW_SIZES)
    v_far = exchange(s_far, tbl[T_SEND + 3], "row", FAR_PAIRS, ROW_SIZES)
    prop = jnp.stack([jnp.cos(prop_phase), jnp.sin(prop_phase)])
    return pl.pallas_call(
        sweeps,
        out_shape=shape(4, TILE, TILE),
        in_specs=[SMEM, VMEM, VMEM, VMEM, VMEM] + [ANY] * 5,
        out_specs=VMEM,
        scratch_shapes=[
            pltpu.VMEM((36, 5, S, S), F32),
            pltpu.VMEM((12, 768, 768), F32),
            pltpu.SemaphoreType.DMA((36,)),
        ],
        compiler_params=PARAMS,
        name="sweeps",
    )(tbl, object_tiles, probe, prop, jnp.asarray(wave_tables()), own, h_near, h_far, v_near, v_far)


def solution(mesh):
    return jax.shard_map(
        on_device,
        mesh=mesh,
        in_specs=(
            P(None, "row", "col"),
            P(),
            P(),
            P(None, "row", "col"),
            P("row", "col", None, None),
            P("row", "col"),
        ),
        out_specs=P(None, "row", "col"),
        check_vma=False,
    )
```

```python
import jax
import jax.numpy as jnp
import numpy as np
from jax import lax
from jax.experimental import pallas as pl
from jax.experimental.pallas import tpu as pltpu
from jax.sharding import PartitionSpec as P

S = 128
HALF = 64
TILE = 256
SLOTS = 4
LONG = S + 8
GROUP = 4
FAR = 1 << 20
LIMIT = 56 * 1024 * 1024
F32 = jnp.float32
I32 = jnp.int32

NEAR_UP = [(i, i + 1) for i in range(0, 16, 2)]
NEAR_DOWN = [(j, i) for i, j in NEAR_UP]
FAR_UP = [(i, i + 1) for i in range(1, 15, 2)]
FAR_DOWN = [(j, i) for i, j in FAR_UP]
ROW_SIZES = (2, 3, 4, 5, 6, 8, 12)
COL_SIZES = (1, 2, 3, 4, 5, 6, 8, 12)
CHIP_SIZES = (2, 4, 12)

T_SEND = 0
T_N0 = 4
T_N1 = 5
T_NH = 6
T_ROW = 8
T_NV = 10
T_PIECE = 12
T_COL = 24
T_CAME = 48
T_LIST1 = 80
T_MAIN = 128
T_SIZE = 384


def wave_tables():
    index = np.arange(S)
    phase = (index[:, None] * index[None, :] % S) * (2.0 * np.pi / S)
    cosine = np.cos(phase) / np.sqrt(S)
    sine = np.sin(phase) / np.sqrt(S)
    first = np.block([[cosine, sine], [-sine, cosine]])
    second = np.block([[cosine, -sine], [sine, cosine]])
    return np.stack([first, second]).astype(jnp.bfloat16)


def roll(x, by):
    return pltpu.roll(x, by, 1)


def pack_cols(info, tile, near, far):
    lane = lax.broadcasted_iota(I32, (TILE, 128), 1)
    low = lane < HALF
    odd = (lane * 0 + info[9]) == 1
    for q in range(2):
        a0, a1 = tile[2 * q, :, 0:128], tile[2 * q, :, 128:256]
        b0, b1 = tile[2 * q + 1, :, 0:128], tile[2 * q + 1, :, 128:256]
        left = jnp.where(low, a0, roll(b0, HALF))
        right = jnp.where(low, roll(a1, HALF), b1)
        rows = slice(q * TILE, (q + 1) * TILE)
        near[rows, :] = jnp.where(odd, left, right)
        far[rows, :] = jnp.where(odd, right, left)


def tile_touch(r, c, row0, col0):
    return (r < row0 + TILE) & (r + S > row0) & (c < col0 + TILE) & (c + S > col0)


def pick(ref, lead, r, c, lane):
    line = pl.multiple_of((r // 8) * 8, 8)
    block = pl.multiple_of((c // 128) * 128, 128)
    rest = c % 128
    step = r % 8
    back = (128 - rest) % 128
    one = roll(ref[lead, pl.ds(line, LONG), pl.ds(block, 128)], back)
    two = roll(ref[lead, pl.ds(line, LONG), pl.ds(block + 128, 128)], back)
    wide = jnp.where(lane < 128 - rest, one, two).reshape(LONG // 8, 8, 128)
    wide = pltpu.roll(wide, (8 - step) % 8, 1)
    sub = lax.broadcasted_iota(I32, (S // 8, 8, 128), 1)
    return jnp.where(sub < 8 - step, wide[:-1], wide[1:]).reshape(S, 128)


def put(ref, lead, r, c, value, lane):
    line = pl.multiple_of((r // 8) * 8, 8)
    block = pl.multiple_of((c // 128) * 128, 128)
    rest = c % 128
    step = r % 8
    moved = pltpu.roll(roll(value, rest).reshape(S // 8, 8, 128), step, 1)
    sub = lax.broadcasted_iota(I32, (LONG // 8, 8, 128), 1)
    none = jnp.zeros((1, 8, 128), F32)
    moved = jnp.where(sub >= step, jnp.concatenate([moved, none]), jnp.concatenate([none, moved])).reshape(LONG, 128)
    zero = jnp.zeros_like(moved)
    ref[lead, pl.ds(line, LONG), pl.ds(block, 128)] += jnp.where(lane >= rest, moved, zero)
    ref[lead, pl.ds(line, LONG), pl.ds(block + 128, 128)] += jnp.where(lane < rest, moved, zero)


def branch_of(sent, got, lower, sizes, kinds):
    most = jnp.maximum(sent, got)
    step = jnp.int32(1)
    for size in sizes[:-1]:
        step = step + jnp.where(most > size, 1, 0)
    up = jnp.where(lower, sent, got)
    down = jnp.where(lower, got, sent)
    kind = jnp.where(down == 0, 1, jnp.where(up == 0, 2, 0)) if kinds == 3 else 0
    return jnp.where(most == 0, 0, kinds * (step - 1) + 1 + kind)


def plan(
    info, tile, near, far, middle, meta_near, meta_far, amps,
    wide, own, s_near, s_far, tbl, ext, vec, meta_s, need_s, sems,
):
    lane8 = lax.broadcasted_iota(I32, (8, 128), 1)
    odd8 = (lane8 * 0 + info[9]) == 1
    vec[0:8, :] = jnp.where(odd8, meta_near[...], meta_far[...]).astype(I32)
    vec[8:16, :] = middle[...].astype(I32)
    vec[16:24, :] = jnp.where(odd8, meta_far[...], meta_near[...]).astype(I32)
    copy = pltpu.make_async_copy(vec, meta_s, sems.at[0])
    copy.start()

    lane = lax.broadcasted_iota(I32, (TILE, 128), 1)
    low = lane < HALF
    odd = (lane * 0 + info[9]) == 1
    for q in range(2):
        rows = slice(q * TILE, (q + 1) * TILE)
        left = jnp.where(odd, near[rows, :], far[rows, :])
        right = jnp.where(odd, far[rows, :], near[rows, :])
        for k in range(2):
            p = 2 * q + k
            t0, t1 = roll(tile[p, :, 0:128], HALF), roll(tile[p, :, 128:256], HALF)
            lft = left if k == 0 else roll(left, HALF)
            rgt = roll(right, HALF) if k == 0 else right
            parts = (jnp.where(low, lft, t0), jnp.where(low, t0, t1), jnp.where(low, t1, rgt))
            for b in range(3):
                wide[p, :, b * 128 : (b + 1) * 128] = parts[b]
                ext[p, S : S + TILE, b * 128 : (b + 1) * 128] = parts[b]
    copy.wait()

    def spot(j):
        t, s = j // SLOTS, j % SLOTS
        at = (t % 3) * 8 + t // 3
        return (
            meta_s[at, 1 + 2 * s] + (t // 3 - 1) * TILE,
            meta_s[at, 2 + 2 * s] + (t % 3 - 1) * TILE,
            jnp.where(s < meta_s[at, 0], 1, 0),
        )

    lane = lax.broadcasted_iota(I32, (16, 128), 1)
    tile_row = lax.broadcasted_iota(I32, (16, 128), 0)
    row0 = (tile_row // 3 - 1) * TILE
    col0 = (tile_row % 3 - 1) * TILE
    rows_v = jnp.full((16, 128), FAR, I32)
    cols_v = jnp.full((16, 128), FAR, I32)
    where_r, where_c = [], []
    for j in range(36):
        r, c, used = spot(j)
        r = jnp.where(used == 1, r, FAR)
        where_r.append(r)
        where_c.append(c)
        rows_v = jnp.where(lane == j, r, rows_v)
        cols_v = jnp.where(lane == j, c, cols_v)
    need = tile_touch(rows_v, cols_v, row0, col0)
    for j in range(36):
        r, c = where_r[j], where_c[j]
        over = (rows_v - r < S) & (r - rows_v < S) & (cols_v - c < S) & (c - cols_v < S)
        need = need | (tile_touch(r, c, row0, col0) & over)
    there_row = tile_row // 3 - 1 + info[11]
    there_col = tile_row % 3 - 1 + info[12]
    inside = (there_row >= 0) & (there_row < 16) & (there_col >= 0) & (there_col < 16)
    vec[0:16, :] = jnp.where(need & inside & (rows_v < FAR), 1, 0)
    copy = pltpu.make_async_copy(vec.at[0:16], need_s, sems.at[0])
    copy.start()
    lane_s = lax.broadcasted_iota(I32, (LONG, S), 1)
    for s in range(SLOTS):

        @pl.when(s < info[0])
        def _():
            r = info[1 + 2 * s] + S
            c = info[2 + 2 * s] + HALF
            for p in range(4):
                own[s, p] = pick(ext, p, r, c, lane_s)
            own[s, 4] = amps[s]

    copy.wait()

    side_near = 1 - 2 * info[9]
    row_near = 1 - 2 * info[10]
    for k in (T_N0, T_N1, T_NH, T_NH + 1, T_NV):
        tbl[k] = 0
    tbl[T_ROW] = info[11] * TILE
    tbl[T_ROW + 1] = info[12] * TILE

    def add_main(buf, pos, r, c):
        n0 = tbl[T_N0]
        tbl[T_MAIN + 4 * n0] = buf
        tbl[T_MAIN + 4 * n0 + 1] = pos
        tbl[T_MAIN + 4 * n0 + 2] = r
        tbl[T_MAIN + 4 * n0 + 3] = c
        tbl[T_N0] = n0 + 1

        @pl.when(tile_touch(r, c, 0, 0))
        def _():
            n1 = tbl[T_N1]
            tbl[T_LIST1 + n1] = n0
            tbl[T_N1] = n1 + 1

    def add_send(j, slot):
        for e, side in enumerate((side_near, -side_near)):

            @pl.when(need_s[4 + side, j] == 1)
            def _():
                n = tbl[T_NH + e]
                tbl[T_COL + 12 * e + n] = slot
                tbl[T_NH + e] = n + 1

    def wanted(j, up):
        t = 4 + 3 * up
        return need_s[t - 1, j] | need_s[t, j] | need_s[t + 1, j]

    sent = []
    for up, buf in ((row_near, s_near), (-row_near, s_far)):
        count = jnp.int32(0)
        for s in range(SLOTS):
            flag = wanted(16 + s, up)

            @pl.when(flag == 1)
            def _():
                for p in range(5):
                    buf[count, p] = own[s, p, 0:HALF, :]
                    buf[count + 1, p] = own[s, p, HALF:S, :]

            count = count + 2 * flag
        for s in range(SLOTS):
            r, c, used = spot(4 + s)
            r_low, c_low, used_low = spot(28 + s)
            r = jnp.where(up == 1, r_low, r)
            c = jnp.where(up == 1, c_low, c)
            used = jnp.where(up == 1, used_low, used)
            flag = jnp.where((used == 1) & (r < TILE) & (r + S > 0), 1, 0)

            @pl.when(flag == 1)
            def _():
                for p in range(4):
                    got = pick(ext, p, r + S, c + HALF, lane_s)
                    buf[count, p] = jnp.where(up == 1, got[0:HALF], got[HALF:S])

            count = count + flag
        sent.append(count)
    for s in range(SLOTS):

        @pl.when(s < info[0])
        def _():
            add_main(0, s, info[1 + 2 * s], info[2 + 2 * s])
            add_send(16 + s, s)

    got = []
    for up in (-1, 1):
        buf = jnp.where(row_near == up, 0, 1)
        count = jnp.int32(0)
        for s in range(SLOTS):
            j = (4 + 3 * up) * SLOTS + s
            flag = need_s[3, j] | need_s[4, j] | need_s[5, j]

            @pl.when(flag == 1)
            def _():
                r, c, _ = spot(j)
                n = tbl[T_NV]
                tbl[T_CAME + 4 * n] = buf
                tbl[T_CAME + 4 * n + 1] = count
                tbl[T_CAME + 4 * n + 2] = r
                tbl[T_CAME + 4 * n + 3] = c
                tbl[T_NV] = n + 1

                @pl.when(need_s[4, j] == 1)
                def _():
                    add_main(0, SLOTS + n, r, c)

                add_send(j, SLOTS + n)

            count = count + 2 * flag
        for s in range(SLOTS):
            r = info[1 + 2 * s]
            out = (r < 0) if up == -1 else (r + S > TILE)
            there = info[11] + up
            flag = jnp.where((s < info[0]) & out & (there >= 0) & (there < 16), 1, 0)
            tbl[T_PIECE + 2 * s + (up + 1) // 2] = jnp.where(flag == 1, count, -1)
            count = count + flag
        got.append(count)
    got_near = jnp.where(row_near == 1, got[1], got[0])
    got_far = jnp.where(row_near == 1, got[0], got[1])
    tbl[T_SEND] = branch_of(sent[0], got_near, info[10] == 0, ROW_SIZES, 3)
    tbl[T_SEND + 1] = branch_of(sent[1], got_far, info[10] == 1, ROW_SIZES, 3)

    got = []
    for side in (-1, 1):
        buf = jnp.where(side_near == side, 1, 2)
        count = jnp.int32(0)
        for t in (4 + side, 1 + side, 7 + side):
            for s in range(SLOTS):
                j = t * SLOTS + s
                flag = need_s[4, j]

                @pl.when(flag == 1)
                def _():
                    r, c, _ = spot(j)
                    add_main(buf, count, r, c)

                count = count + flag
        got.append(count)
    got_near = jnp.where(side_near == 1, got[1], got[0])
    got_far = jnp.where(side_near == 1, got[0], got[1])
    tbl[T_SEND + 2] = branch_of(tbl[T_NH], got_near, info[9] == 0, CHIP_SIZES, 1)
    tbl[T_SEND + 3] = branch_of(tbl[T_NH + 1], got_far, info[9] == 1, COL_SIZES, 3)


def merge(info, tbl, wide, own, v_near, v_far, out, h_near, h_far, ext, rec, sems):
    copy = pltpu.make_async_copy(wide, ext.at[:, S : S + TILE], sems.at[0])
    copy.start()
    high = lax.broadcasted_iota(I32, (S, S), 0)
    lane = lax.broadcasted_iota(I32, (LONG, S), 1)

    def half(far, unit, p):
        return jnp.where(far == 1, v_far[unit, p], v_near[unit, p])

    for s in range(SLOTS):

        @pl.when(s < info[0])
        def _():
            for p in range(5):
                rec[s, p] = own[s, p]
            r = info[1 + 2 * s]
            above, below = tbl[T_PIECE + 2 * s], tbl[T_PIECE + 2 * s + 1]
            top = high[0:HALF] + r < 0
            bottom = high[HALF:S] + r >= TILE
            zero = jnp.zeros((HALF, S), F32)

            @pl.when(r < 0)
            def _():
                for p in range(4):
                    part = jnp.where(above >= 0, half(1 - info[10], jnp.maximum(above, 0), p), zero)
                    rec[s, p, 0:HALF] = jnp.where(top, part, rec[s, p, 0:HALF])

            @pl.when(r + S > TILE)
            def _():
                for p in range(4):
                    part = jnp.where(below >= 0, half(info[10], jnp.maximum(below, 0), p), zero)
                    rec[s, p, HALF:S] = jnp.where(bottom, part, rec[s, p, HALF:S])

    copy.wait()

    @pl.loop(0, tbl[T_NV])
    def _(i):
        far = tbl[T_CAME + 4 * i]
        unit = tbl[T_CAME + 4 * i + 1]
        r = tbl[T_CAME + 4 * i + 2]
        c = tbl[T_CAME + 4 * i + 3]
        slot = SLOTS + i
        for p in range(5):
            rec[slot, p, 0:HALF] = half(far, unit, p)
            rec[slot, p, HALF:S] = half(far, unit + 1, p)

        @pl.when((r < TILE) & (r + S > 0))
        def _():
            mine = (high + r >= 0) & (high + r < TILE)
            for p in range(4):
                rec[slot, p] = jnp.where(mine, pick(ext, p, r + S, c + HALF, lane), rec[slot, p])

    came = tbl[T_NV]

    def keep(k):
        return pltpu.make_async_copy(rec.at[k], out.at[k], sems.at[k])

    def send(e, i):
        target = h_near if e == 0 else h_far
        return pltpu.make_async_copy(rec.at[tbl[T_COL + 12 * e + i]], target.at[i], sems.at[12 + 12 * e + i])

    for e in range(2):

        @pl.loop(0, tbl[T_NH + e])
        def _(i):
            send(e, i).start()

    @pl.loop(0, info[0])
    def _(i):
        keep(i).start()

    @pl.loop(SLOTS, SLOTS + came)
    def _(i):
        keep(i).start()

    for e in range(2):

        @pl.loop(0, tbl[T_NH + e])
        def _(i):
            send(e, i).wait()

    @pl.loop(0, info[0])
    def _(i):
        keep(i).wait()

    @pl.loop(SLOTS, SLOTS + came)
    def _(i):
        keep(i).wait()


def times(a, b):
    return (a[0] * b[0] - a[1] * b[1], a[0] * b[1] + a[1] * b[0])


def conj_times(a, b):
    return (a[0] * b[0] + a[1] * b[1], a[0] * b[1] - a[1] * b[0])


def transform(x, left, right):
    return [y for k in range(0, GROUP, 2) for y in transform_pair(x[k : k + 2], left, right)]


def transform_pair(x, left, right):
    half = [jnp.concatenate([w[k].astype(jnp.bfloat16) for w in x], axis=1) for k in range(2)]
    half = jnp.concatenate(half, axis=0)
    half = jnp.dot(left, half, preferred_element_type=F32).astype(jnp.bfloat16)
    half = [jnp.concatenate([half[:S, at], half[S:, at]], axis=1) for at in (slice(0, S), slice(S, 2 * S))]
    done = jnp.dot(jnp.concatenate(half, axis=0), right, preferred_element_type=F32)
    return [(done[at, :S], done[at, S:]) for at in (slice(0, S), slice(S, 2 * S))]


def sweeps(tbl, tile, probe, prop, waves, own, h_near, h_far, out, rec, acc, sems):
    n0 = tbl[T_N0]
    n1 = tbl[T_N1]

    @pl.loop(0, n0)
    def _(i):
        buf = tbl[T_MAIN + 4 * i]
        pos = tbl[T_MAIN + 4 * i + 1]
        for b, source in enumerate((own, h_near, h_far)):

            @pl.when(buf == b)
            def _():
                pltpu.make_async_copy(source.at[pos], rec.at[i], sems.at[i]).start()

    @pl.loop(0, 12)
    def _(p):
        acc[p, 128:640, 128:640] = jnp.zeros((512, 512), F32)

    lane = lax.broadcasted_iota(I32, (LONG, S), 1)
    def group(i, base, count, second):
        at = []
        for k in range(GROUP):
            place = GROUP * i + k
            there = place < count
            e = tbl[T_LIST1 + jnp.minimum(place, 35)] if second else place
            e = jnp.where(there, e, 36)
            r = jnp.where(there, tbl[T_MAIN + 4 * e + 2] + TILE, 5 * S)
            c = jnp.where(there, tbl[T_MAIN + 4 * e + 3] + TILE, 0)
            at.append((e, r, c))
            if second:
                high = tbl[T_ROW] + r - TILE + lax.broadcasted_iota(I32, (S, S), 0)
                wide = tbl[T_ROW + 1] + c - TILE + lax.broadcasted_iota(I32, (S, S), 1)
                inside = (high >= 0) & (high < 16 * TILE) & (wide >= 0) & (wide < 16 * TILE)
                for m in range(2):
                    scale = jnp.where(inside, 1.0 / (pick(acc, 4 + m, r, c, lane) + 1.0), 0.0)
                    for p in (2 * m, 2 * m + 1):
                        rec[e, p] = rec[e, p] - pick(acc, p, r, c, lane) * scale
            else:

                @pl.when(there)
                def _():
                    pltpu.make_async_copy(own.at[0], rec.at[e], sems.at[e]).wait()

        wave = (probe[0], probe[1])
        spread = (prop[0], prop[1])
        one, two = waves[0], waves[1]
        exits = [times(wave, (rec[e, 0], rec[e, 1])) for e, _, _ in at]
        inner = transform([times(spread, x) for x in transform(exits, one, two)], two, one)
        o2 = [(rec[e, 2], rec[e, 3]) for e, _, _ in at]
        field = transform([times(x, o) for x, o in zip(inner, o2)], one, two)
        chi = []
        for (e, _, _), f in zip(at, field):
            size = jnp.sqrt(f[0] * f[0] + f[1] * f[1])
            keep = 1.0 - rec[e, 4] / jnp.maximum(size, 1.0)
            chi.append((f[0] * keep, f[1] * keep))
        g2 = transform(chi, two, one)
        for (_, r, c), x, g in zip(at, inner, g2):
            later = conj_times(x, g)
            put(acc, base + 2, r, c, later[0], lane)
            put(acc, base + 3, r, c, later[1], lane)
            put(acc, base + 5, r, c, x[0] * x[0] + x[1] * x[1], lane)
        back = transform([conj_times(o, g) for o, g in zip(o2, g2)], one, two)
        first = transform([conj_times(spread, x) for x in back], two, one)
        light = wave[0] * wave[0] + wave[1] * wave[1]
        for (_, r, c), g in zip(at, first):
            low = conj_times(wave, g)
            put(acc, base, r, c, low[0], lane)
            put(acc, base + 1, r, c, low[1], lane)
            put(acc, base + 4, r, c, light, lane)

    @pl.loop(0, (n0 + GROUP - 1) // GROUP)
    def _(i):
        group(i, 0, n0, False)

    @pl.loop(0, (n1 + GROUP - 1) // GROUP)
    def _(i):
        group(i, 6, n1, True)

    for k in range(2):
        one = 1.0 / (acc[4 + k, 256:512, 256:512] + 1.0)
        two = 1.0 / (acc[10 + k, 256:512, 256:512] + 1.0)
        for p in (2 * k, 2 * k + 1):
            out[p] = tile[p] - acc[p, 256:512, 256:512] * one - acc[6 + p, 256:512, 256:512] * two


VMEM = pl.BlockSpec(memory_space=pltpu.VMEM)
SMEM = pl.BlockSpec(memory_space=pltpu.SMEM)
ANY = pl.BlockSpec(memory_space=pl.ANY)
PARAMS = pltpu.CompilerParams(vmem_limit_bytes=LIMIT)


def shape(*dims, dtype=F32):
    return jax.ShapeDtypeStruct(dims, dtype)


def records(count):
    return shape(count, 5, S, S)


def nothing(out):
    pass


def exchange(sent, branch, axis, ups, downs, sizes, kinds=3):
    full = sent.shape[0]

    def blank():
        return pl.pallas_call(nothing, out_shape=shape(*sent.shape), out_specs=ANY, name="blank")()

    def of(count, pairs):
        def run(value):
            got = lax.ppermute(value[:count], axis, pairs)
            return got if count == full else lax.dynamic_update_slice(blank(), got, (0, 0, 0, 0))

        return run

    branches = [lambda value: blank()]
    branches += [of(count, pairs) for count in sizes for pairs in (ups + downs, ups, downs)[:kinds]]
    return lax.switch(branch, branches, sent)


def on_device(object_tiles, probe, prop_phase, amplitudes, offsets, counts):
    row = lax.axis_index("row").astype(I32)
    col = lax.axis_index("col").astype(I32)
    info = jnp.concatenate(
        [counts.reshape(1), offsets.reshape(8), jnp.stack([col % 2, row % 2, row, col]), jnp.zeros((3,), I32)]
    )
    meta = jnp.broadcast_to(jnp.pad(info.astype(F32), (0, 112)), (8, 128))
    meta_far = lax.ppermute(meta, "row", FAR_UP + FAR_DOWN)
    meta_near = lax.ppermute(meta, "row", NEAR_UP + NEAR_DOWN)
    near, far = pl.pallas_call(
        pack_cols,
        out_shape=(shape(512, 128), shape(512, 128)),
        in_specs=[SMEM, VMEM],
        out_specs=(VMEM, VMEM),
        compiler_params=PARAMS,
        name="pack_cols",
    )(info, object_tiles)
    far = lax.ppermute(far, "col", FAR_UP + FAR_DOWN)
    near = lax.ppermute(near, "col", NEAR_UP + NEAR_DOWN)
    line = lax.broadcasted_iota(I32, (8, 128), 0)
    odd = row % 2 == 1
    above = jnp.where(odd, meta_near, meta_far)
    below = jnp.where(odd, meta_far, meta_near)
    middle = jnp.where(line == 0, above, jnp.where(line == 1, meta, below))
    meta_far = lax.ppermute(middle, "col", FAR_UP + FAR_DOWN)
    meta_near = lax.ppermute(middle, "col", NEAR_UP + NEAR_DOWN)
    wide, own, s_near, s_far, tbl = pl.pallas_call(
        plan,
        out_shape=(
            shape(4, TILE, 384),
            records(4),
            shape(12, 5, HALF, S),
            shape(12, 5, HALF, S),
            shape(T_SIZE, dtype=I32),
        ),
        in_specs=[SMEM] + [VMEM] * 7,
        out_specs=(VMEM, VMEM, VMEM, VMEM, SMEM),
        scratch_shapes=[
            pltpu.VMEM((4, 512, 384), F32),
            pltpu.VMEM((24, 128), I32),
            pltpu.SMEM((24, 128), I32),
            pltpu.SMEM((16, 128), I32),
            pltpu.SemaphoreType.DMA((1,)),
        ],
        compiler_params=PARAMS,
        name="plan",
    )(info, object_tiles, near, far, middle, meta_near, meta_far, amplitudes)
    v_far = exchange(s_far, tbl[T_SEND + 1], "row", FAR_UP, FAR_DOWN, ROW_SIZES)
    v_near = exchange(s_near, tbl[T_SEND], "row", NEAR_UP, NEAR_DOWN, ROW_SIZES)
    own, s_near, s_far = pl.pallas_call(
        merge,
        out_shape=(records(12), records(12), records(12)),
        in_specs=[SMEM, SMEM, ANY, VMEM, VMEM, VMEM],
        out_specs=(ANY, ANY, ANY),
        scratch_shapes=[
            pltpu.VMEM((4, 512, 384), F32),
            pltpu.VMEM((12, 5, S, S), F32),
            pltpu.SemaphoreType.DMA((36,)),
        ],
        compiler_params=PARAMS,
        name="merge",
    )(info, tbl, wide, own, v_near, v_far)
    h_far = exchange(s_far, tbl[T_SEND + 3], "col", FAR_UP, FAR_DOWN, COL_SIZES)
    h_near = exchange(s_near, tbl[T_SEND + 2], "col", NEAR_UP, NEAR_DOWN, CHIP_SIZES, 1)
    prop = jnp.stack([jnp.cos(prop_phase), jnp.sin(prop_phase)])
    return pl.pallas_call(
        sweeps,
        out_shape=shape(4, TILE, TILE),
        in_specs=[SMEM, VMEM, VMEM, VMEM, VMEM] + [ANY] * 3,
        out_specs=VMEM,
        scratch_shapes=[
            pltpu.VMEM((37, 5, S, S), F32),
            pltpu.VMEM((12, 776, 768), F32),
            pltpu.SemaphoreType.DMA((36,)),
        ],
        compiler_params=PARAMS,
        name="sweeps",
    )(tbl, object_tiles, probe, prop, jnp.asarray(wave_tables()), own, h_near, h_far)


def solution(mesh):
    return jax.shard_map(
        on_device,
        mesh=mesh,
        in_specs=(
            P(None, "row", "col"),
            P(),
            P(),
            P(None, "row", "col"),
            P("row", "col", None, None),
            P("row", "col"),
        ),
        out_specs=P(None, "row", "col"),
        check_vma=False,
    )
```

```python
import jax
import jax.numpy as jnp
import numpy as np
from jax import lax
from jax.experimental import pallas as pl
from jax.experimental.pallas import tpu as pltpu
from jax.sharding import PartitionSpec as P

S = 128
HALF = 64
TILE = 256
SLOTS = 4
LONG = S + 8
GROUP = 4
FAR = 1 << 20
LIMIT = 56 * 1024 * 1024
F32 = jnp.float32
I32 = jnp.int32

NEAR_UP = [(i, i + 1) for i in range(0, 16, 2)]
NEAR_DOWN = [(j, i) for i, j in NEAR_UP]
FAR_UP = [(i, i + 1) for i in range(1, 15, 2)]
FAR_DOWN = [(j, i) for i, j in FAR_UP]
ROW_SIZES = (2, 3, 4, 5, 6, 8, 12)
COL_SIZES = (1, 2, 3, 4, 5, 6, 8, 12)
CHIP_SIZES = (2, 4, 12)

T_N0 = 4
T_N1 = 5
T_NH = 6
T_ROW = 8
T_UNIT = 11
T_NV = 10
T_PIECE = 12
T_COL = 24
T_CAME = 48
T_LIST1 = 80
T_MAIN = 128
T_SIZE = 384


def wave_tables():
    index = np.arange(S)
    phase = (index[:, None] * index[None, :] % S) * (2.0 * np.pi / S)
    cosine = np.cos(phase) / np.sqrt(S)
    sine = np.sin(phase) / np.sqrt(S)
    first = np.block([[cosine, sine], [-sine, cosine]])
    second = np.block([[cosine, -sine], [sine, cosine]])
    return np.stack([first, second]).astype(jnp.bfloat16)


def roll(x, by):
    return pltpu.roll(x, by, 1)


def pack_cols(info, tile, near, far, meta):
    lane = lax.broadcasted_iota(I32, (TILE, 128), 1)
    low = lane < HALF
    odd = (lane * 0 + info[9]) == 1
    for q in range(2):
        a0, a1 = tile[2 * q, :, 0:128], tile[2 * q, :, 128:256]
        b0, b1 = tile[2 * q + 1, :, 0:128], tile[2 * q + 1, :, 128:256]
        left = jnp.where(low, a0, roll(b0, HALF))
        right = jnp.where(low, roll(a1, HALF), b1)
        rows = slice(q * TILE, (q + 1) * TILE)
        near[rows, :] = jnp.where(odd, left, right)
        far[rows, :] = jnp.where(odd, right, left)
    lane = lax.broadcasted_iota(I32, (8, 128), 1)
    mine = jnp.zeros((8, 128), I32)
    for k in range(9):
        mine = jnp.where(lane == k, info[k], mine)
    meta[...] = mine.astype(F32)


def tile_touch(r, c, row0, col0):
    return (r < row0 + TILE) & (r + S > row0) & (c < col0 + TILE) & (c + S > col0)


def pick(ref, lead, r, c, lane):
    line = pl.multiple_of((r // 8) * 8, 8)
    block = pl.multiple_of((c // 128) * 128, 128)
    rest = c % 128
    step = r % 8
    back = (128 - rest) % 128
    one = roll(ref[lead, pl.ds(line, LONG), pl.ds(block, 128)], back)
    two = roll(ref[lead, pl.ds(line, LONG), pl.ds(block + 128, 128)], back)
    wide = jnp.where(lane < 128 - rest, one, two).reshape(LONG // 8, 8, 128)
    wide = pltpu.roll(wide, (8 - step) % 8, 1)
    sub = lax.broadcasted_iota(I32, (S // 8, 8, 128), 1)
    return jnp.where(sub < 8 - step, wide[:-1], wide[1:]).reshape(S, 128)


def put(ref, lead, r, c, value, lane):
    line = pl.multiple_of((r // 8) * 8, 8)
    block = pl.multiple_of((c // 128) * 128, 128)
    rest = c % 128
    step = r % 8
    moved = pltpu.roll(roll(value, rest).reshape(S // 8, 8, 128), step, 1)
    sub = lax.broadcasted_iota(I32, (LONG // 8, 8, 128), 1)
    none = jnp.zeros((1, 8, 128), F32)
    moved = jnp.where(sub >= step, jnp.concatenate([moved, none]), jnp.concatenate([none, moved])).reshape(LONG, 128)
    zero = jnp.zeros_like(moved)
    ref[lead, pl.ds(line, LONG), pl.ds(block, 128)] += jnp.where(lane >= rest, moved, zero)
    ref[lead, pl.ds(line, LONG), pl.ds(block + 128, 128)] += jnp.where(lane < rest, moved, zero)


def branch_of(sent, got, lower, sizes, kinds):
    most = jnp.maximum(sent, got)
    step = jnp.int32(1)
    for size in sizes[:-1]:
        step = step + jnp.where(most > size, 1, 0)
    up = jnp.where(lower, sent, got)
    down = jnp.where(lower, got, sent)
    kind = jnp.where(down == 0, 1, jnp.where(up == 0, 2, 0)) if kinds == 3 else 0
    return jnp.where(most == 0, 0, kinds * (step - 1) + 1 + kind)


def plan(
    info, tile, near, far, middle, meta_near, meta_far, amps,
    wide, own, s_near, s_far, tbl, b0, b1, b2, b3, ext, vec, meta_s, need_s, sems,
):
    lane8 = lax.broadcasted_iota(I32, (8, 128), 1)
    odd8 = (lane8 * 0 + info[9]) == 1
    vec[0:8, :] = jnp.where(odd8, meta_near[...], meta_far[...]).astype(I32)
    vec[8:16, :] = middle[...].astype(I32)
    vec[16:24, :] = jnp.where(odd8, meta_far[...], meta_near[...]).astype(I32)
    copy = pltpu.make_async_copy(vec, meta_s, sems.at[0])
    copy.start()

    lane = lax.broadcasted_iota(I32, (TILE, 128), 1)
    low = lane < HALF
    odd = (lane * 0 + info[9]) == 1
    for q in range(2):
        rows = slice(q * TILE, (q + 1) * TILE)
        left = jnp.where(odd, near[rows, :], far[rows, :])
        right = jnp.where(odd, far[rows, :], near[rows, :])
        for k in range(2):
            p = 2 * q + k
            t0, t1 = roll(tile[p, :, 0:128], HALF), roll(tile[p, :, 128:256], HALF)
            lft = left if k == 0 else roll(left, HALF)
            rgt = roll(right, HALF) if k == 0 else right
            parts = (jnp.where(low, lft, t0), jnp.where(low, t0, t1), jnp.where(low, t1, rgt))
            for b in range(3):
                wide[p, :, b * 128 : (b + 1) * 128] = parts[b]
                ext[p, S : S + TILE, b * 128 : (b + 1) * 128] = parts[b]
    copy.wait()

    def spot(j):
        t, s = j // SLOTS, j % SLOTS
        at = (t % 3) * 8 + t // 3
        return (
            meta_s[at, 1 + 2 * s] + (t // 3 - 1) * TILE,
            meta_s[at, 2 + 2 * s] + (t % 3 - 1) * TILE,
            jnp.where(s < meta_s[at, 0], 1, 0),
        )

    lane = lax.broadcasted_iota(I32, (16, 128), 1)
    tile_row = lax.broadcasted_iota(I32, (16, 128), 0)
    row0 = (tile_row // 3 - 1) * TILE
    col0 = (tile_row % 3 - 1) * TILE
    rows_v = jnp.full((16, 128), FAR, I32)
    cols_v = jnp.full((16, 128), FAR, I32)
    where_r, where_c = [], []
    for j in range(36):
        r, c, used = spot(j)
        r = jnp.where(used == 1, r, FAR)
        where_r.append(r)
        where_c.append(c)
        rows_v = jnp.where(lane == j, r, rows_v)
        cols_v = jnp.where(lane == j, c, cols_v)
    need = tile_touch(rows_v, cols_v, row0, col0)
    for j in range(36):
        r, c = where_r[j], where_c[j]
        over = (rows_v - r < S) & (r - rows_v < S) & (cols_v - c < S) & (c - cols_v < S)
        need = need | (tile_touch(r, c, row0, col0) & over)
    there_row = tile_row // 3 - 1 + info[11]
    there_col = tile_row % 3 - 1 + info[12]
    inside = (there_row >= 0) & (there_row < 16) & (there_col >= 0) & (there_col < 16)
    vec[0:16, :] = jnp.where(need & inside & (rows_v < FAR), 1, 0)
    copy = pltpu.make_async_copy(vec.at[0:16], need_s, sems.at[0])
    copy.start()
    lane_s = lax.broadcasted_iota(I32, (LONG, S), 1)

    @pl.loop(0, info[0])
    def _(s):
        r = info[1 + 2 * s] + S
        c = info[2 + 2 * s] + HALF
        for p in range(4):
            own[s, p] = pick(ext, p, r, c, lane_s)
        own[s, 4] = amps[s]

    copy.wait()

    side_near = 1 - 2 * info[9]
    row_near = 1 - 2 * info[10]
    for k in (T_N0, T_N1, T_NH, T_NH + 1, T_NV):
        tbl[k] = 0
    tbl[T_ROW] = info[11] * TILE
    tbl[T_ROW + 1] = info[12] * TILE

    def add_main(buf, pos, r, c):
        n0 = tbl[T_N0]
        tbl[T_MAIN + 4 * n0] = buf
        tbl[T_MAIN + 4 * n0 + 1] = pos
        tbl[T_MAIN + 4 * n0 + 2] = r
        tbl[T_MAIN + 4 * n0 + 3] = c
        tbl[T_N0] = n0 + 1

        @pl.when(tile_touch(r, c, 0, 0))
        def _():
            n1 = tbl[T_N1]
            tbl[T_LIST1 + n1] = n0
            tbl[T_N1] = n1 + 1

    def add_send(j, slot):
        for e, side in enumerate((side_near, -side_near)):

            @pl.when(need_s[4 + side, j] == 1)
            def _():
                n = tbl[T_NH + e]
                tbl[T_COL + 12 * e + n] = slot
                tbl[T_NH + e] = n + 1

    def wanted(j, up):
        t = 4 + 3 * up
        return need_s[t - 1, j] | need_s[t, j] | need_s[t + 1, j]

    sent = []
    for up, buf in ((row_near, s_near), (-row_near, s_far)):
        count = jnp.int32(0)
        for s in range(SLOTS):
            flag = wanted(16 + s, up)

            @pl.when(flag == 1)
            def _():
                for p in range(5):
                    buf[count, p] = own[s, p, 0:HALF, :]
                    buf[count + 1, p] = own[s, p, HALF:S, :]

            count = count + 2 * flag
        tbl[T_UNIT] = count

        @pl.loop(0, meta_s[9 + up, 0])
        def _(s):
            r = meta_s[9 + up, 1 + 2 * s] + up * TILE
            c = meta_s[9 + up, 2 + 2 * s]

            @pl.when((r < TILE) & (r + S > 0))
            def _():
                count = tbl[T_UNIT]
                for p in range(4):
                    got = pick(ext, p, r + S, c + HALF, lane_s)
                    buf[count, p] = jnp.where(up == 1, got[0:HALF], got[HALF:S])
                tbl[T_UNIT] = count + 1

        sent.append(tbl[T_UNIT])
    for s in range(SLOTS):

        @pl.when(s < info[0])
        def _():
            add_main(0, s, info[1 + 2 * s], info[2 + 2 * s])
            add_send(16 + s, s)

    got = []
    for up in (-1, 1):
        buf = jnp.where(row_near == up, 0, 1)
        count = jnp.int32(0)
        for s in range(SLOTS):
            j = (4 + 3 * up) * SLOTS + s
            flag = need_s[3, j] | need_s[4, j] | need_s[5, j]

            @pl.when(flag == 1)
            def _():
                r, c, _ = spot(j)
                n = tbl[T_NV]
                tbl[T_CAME + 4 * n] = buf
                tbl[T_CAME + 4 * n + 1] = count
                tbl[T_CAME + 4 * n + 2] = r
                tbl[T_CAME + 4 * n + 3] = c
                tbl[T_NV] = n + 1

                @pl.when(need_s[4, j] == 1)
                def _():
                    add_main(0, SLOTS + n, r, c)

                add_send(j, SLOTS + n)

            count = count + 2 * flag
        for s in range(SLOTS):
            r = info[1 + 2 * s]
            out = (r < 0) if up == -1 else (r + S > TILE)
            there = info[11] + up
            flag = jnp.where((s < info[0]) & out & (there >= 0) & (there < 16), 1, 0)
            tbl[T_PIECE + 2 * s + (up + 1) // 2] = jnp.where(flag == 1, count, -1)
            count = count + flag
        got.append(count)
    got_near = jnp.where(row_near == 1, got[1], got[0])
    got_far = jnp.where(row_near == 1, got[0], got[1])
    b0[0] = branch_of(sent[0], got_near, info[10] == 0, ROW_SIZES, 1)
    b1[0] = branch_of(sent[1], got_far, info[10] == 1, ROW_SIZES, 1)

    got = []
    for side in (-1, 1):
        buf = jnp.where(side_near == side, 1, 2)
        count = jnp.int32(0)
        for t in (4 + side, 1 + side, 7 + side):
            for s in range(SLOTS):
                j = t * SLOTS + s
                flag = need_s[4, j]

                @pl.when(flag == 1)
                def _():
                    r, c, _ = spot(j)
                    add_main(buf, count, r, c)

                count = count + flag
        got.append(count)
    got_near = jnp.where(side_near == 1, got[1], got[0])
    got_far = jnp.where(side_near == 1, got[0], got[1])
    b2[0] = branch_of(tbl[T_NH], got_near, info[9] == 0, CHIP_SIZES, 1)
    b3[0] = branch_of(tbl[T_NH + 1], got_far, info[9] == 1, COL_SIZES, 3)


def merge(info, tbl, wide, own, v_near, v_far, out, h_near, h_far, ext, rec, sems):
    copy = pltpu.make_async_copy(wide, ext.at[:, S : S + TILE], sems.at[0])
    copy.start()
    high = lax.broadcasted_iota(I32, (S, S), 0)
    lane = lax.broadcasted_iota(I32, (LONG, S), 1)

    def half(far, unit, p):
        return jnp.where(far == 1, v_far[unit, p], v_near[unit, p])

    for s in range(SLOTS):

        @pl.when(s < info[0])
        def _():
            for p in range(5):
                rec[s, p] = own[s, p]
            r = info[1 + 2 * s]
            above, below = tbl[T_PIECE + 2 * s], tbl[T_PIECE + 2 * s + 1]
            top = high[0:HALF] + r < 0
            bottom = high[HALF:S] + r >= TILE
            zero = jnp.zeros((HALF, S), F32)

            @pl.when(r < 0)
            def _():
                for p in range(4):
                    part = jnp.where(above >= 0, half(1 - info[10], jnp.maximum(above, 0), p), zero)
                    rec[s, p, 0:HALF] = jnp.where(top, part, rec[s, p, 0:HALF])

            @pl.when(r + S > TILE)
            def _():
                for p in range(4):
                    part = jnp.where(below >= 0, half(info[10], jnp.maximum(below, 0), p), zero)
                    rec[s, p, HALF:S] = jnp.where(bottom, part, rec[s, p, HALF:S])

    copy.wait()

    @pl.loop(0, tbl[T_NV])
    def _(i):
        far = tbl[T_CAME + 4 * i]
        unit = tbl[T_CAME + 4 * i + 1]
        r = tbl[T_CAME + 4 * i + 2]
        c = tbl[T_CAME + 4 * i + 3]
        slot = SLOTS + i
        for p in range(5):
            rec[slot, p, 0:HALF] = half(far, unit, p)
            rec[slot, p, HALF:S] = half(far, unit + 1, p)

        @pl.when((r < TILE) & (r + S > 0))
        def _():
            mine = (high + r >= 0) & (high + r < TILE)
            for p in range(4):
                rec[slot, p] = jnp.where(mine, pick(ext, p, r + S, c + HALF, lane), rec[slot, p])

    came = tbl[T_NV]

    def keep(k):
        return pltpu.make_async_copy(rec.at[k], out.at[k], sems.at[k])

    def send(e, i):
        target = h_near if e == 0 else h_far
        return pltpu.make_async_copy(rec.at[tbl[T_COL + 12 * e + i]], target.at[i], sems.at[12 + 12 * e + i])

    for e in range(2):

        @pl.loop(0, tbl[T_NH + e])
        def _(i):
            send(e, i).start()

    @pl.loop(0, info[0])
    def _(i):
        keep(i).start()

    @pl.loop(SLOTS, SLOTS + came)
    def _(i):
        keep(i).start()

    for e in range(2):

        @pl.loop(0, tbl[T_NH + e])
        def _(i):
            send(e, i).wait()

    @pl.loop(0, info[0])
    def _(i):
        keep(i).wait()

    @pl.loop(SLOTS, SLOTS + came)
    def _(i):
        keep(i).wait()


def times(a, b):
    return (a[0] * b[0] - a[1] * b[1], a[0] * b[1] + a[1] * b[0])


def conj_times(a, b):
    return (a[0] * b[0] + a[1] * b[1], a[0] * b[1] - a[1] * b[0])


def transform(x, left, right):
    return [y for k in range(0, GROUP, 2) for y in transform_pair(x[k : k + 2], left, right)]


def transform_pair(x, left, right):
    half = [jnp.concatenate([w[k].astype(jnp.bfloat16) for w in x], axis=1) for k in range(2)]
    half = jnp.concatenate(half, axis=0)
    half = jnp.dot(left, half, preferred_element_type=F32).astype(jnp.bfloat16)
    half = [jnp.concatenate([half[:S, at], half[S:, at]], axis=1) for at in (slice(0, S), slice(S, 2 * S))]
    done = jnp.dot(jnp.concatenate(half, axis=0), right, preferred_element_type=F32)
    return [(done[at, :S], done[at, S:]) for at in (slice(0, S), slice(S, 2 * S))]


def sweeps(tbl, tile, probe, prop, waves, own, h_near, h_far, out, rec, acc, sems):
    n0 = tbl[T_N0]
    n1 = tbl[T_N1]

    @pl.loop(0, n0)
    def _(i):
        buf = tbl[T_MAIN + 4 * i]
        pos = tbl[T_MAIN + 4 * i + 1]
        for b, source in enumerate((own, h_near, h_far)):

            @pl.when(buf == b)
            def _():
                pltpu.make_async_copy(source.at[pos], rec.at[i], sems.at[i]).start()

    @pl.loop(0, 12)
    def _(p):
        acc[p, 256:512, 256:512] = jnp.zeros((256, 256), F32)

        @pl.when(p < 6)
        def _():
            acc[p, 128:256, 128:640] = jnp.zeros((128, 512), F32)
            acc[p, 512:640, 128:640] = jnp.zeros((128, 512), F32)
            acc[p, 256:512, 128:256] = jnp.zeros((256, 128), F32)
            acc[p, 256:512, 512:640] = jnp.zeros((256, 128), F32)

    lane = lax.broadcasted_iota(I32, (LONG, S), 1)
    def group(i, base, count, second):
        at = []
        for k in range(GROUP):
            place = GROUP * i + k
            there = place < count
            e = tbl[T_LIST1 + jnp.minimum(place, 35)] if second else place
            e = jnp.where(there, e, 36)
            r = jnp.where(there, tbl[T_MAIN + 4 * e + 2] + TILE, 5 * S)
            c = jnp.where(there, tbl[T_MAIN + 4 * e + 3] + TILE, 0)
            at.append((e, r, c))
            if second:
                high = tbl[T_ROW] + r - TILE + lax.broadcasted_iota(I32, (S, S), 0)
                wide = tbl[T_ROW + 1] + c - TILE + lax.broadcasted_iota(I32, (S, S), 1)
                inside = (high >= 0) & (high < 16 * TILE) & (wide >= 0) & (wide < 16 * TILE)
                for m in range(2):
                    scale = jnp.where(inside, 1.0 / (pick(acc, 4 + m, r, c, lane) + 1.0), 0.0)
                    for p in (2 * m, 2 * m + 1):
                        rec[e, p] = rec[e, p] - pick(acc, p, r, c, lane) * scale
            else:

                @pl.when(there)
                def _():
                    pltpu.make_async_copy(own.at[0], rec.at[e], sems.at[e]).wait()

        wave = (probe[0], probe[1])
        spread = (prop[0], prop[1])
        one, two = waves[0], waves[1]
        exits = [times(wave, (rec[e, 0], rec[e, 1])) for e, _, _ in at]
        inner = transform([times(spread, x) for x in transform(exits, one, two)], two, one)
        o2 = [(rec[e, 2], rec[e, 3]) for e, _, _ in at]
        field = transform([times(x, o) for x, o in zip(inner, o2)], one, two)
        chi = []
        for (e, _, _), f in zip(at, field):
            size = jnp.sqrt(f[0] * f[0] + f[1] * f[1])
            keep = 1.0 - rec[e, 4] / jnp.maximum(size, 1.0)
            chi.append((f[0] * keep, f[1] * keep))
        g2 = transform(chi, two, one)
        for (_, r, c), x, g in zip(at, inner, g2):
            later = conj_times(x, g)
            put(acc, base + 2, r, c, later[0], lane)
            put(acc, base + 3, r, c, later[1], lane)
            put(acc, base + 5, r, c, x[0] * x[0] + x[1] * x[1], lane)
        back = transform([conj_times(o, g) for o, g in zip(o2, g2)], one, two)
        first = transform([conj_times(spread, x) for x in back], two, one)
        light = wave[0] * wave[0] + wave[1] * wave[1]
        for (_, r, c), g in zip(at, first):
            low = conj_times(wave, g)
            put(acc, base, r, c, low[0], lane)
            put(acc, base + 1, r, c, low[1], lane)
            put(acc, base + 4, r, c, light, lane)

    @pl.loop(0, (n0 + GROUP - 1) // GROUP)
    def _(i):
        group(i, 0, n0, False)

    @pl.loop(0, (n1 + GROUP - 1) // GROUP)
    def _(i):
        group(i, 6, n1, True)

    for k in range(2):
        one = 1.0 / (acc[4 + k, 256:512, 256:512] + 1.0)
        two = 1.0 / (acc[10 + k, 256:512, 256:512] + 1.0)
        for p in (2 * k, 2 * k + 1):
            out[p] = tile[p] - acc[p, 256:512, 256:512] * one - acc[6 + p, 256:512, 256:512] * two


VMEM = pl.BlockSpec(memory_space=pltpu.VMEM)
SMEM = pl.BlockSpec(memory_space=pltpu.SMEM)
ANY = pl.BlockSpec(memory_space=pl.ANY)
PARAMS = pltpu.CompilerParams(vmem_limit_bytes=LIMIT)


def shape(*dims, dtype=F32):
    return jax.ShapeDtypeStruct(dims, dtype)


def records(count):
    return shape(count, 5, S, S)


def nothing(out):
    pass


def exchange(sent, branch, axis, ups, downs, sizes, kinds=3):
    full = sent.shape[0]

    def blank():
        return pl.pallas_call(nothing, out_shape=shape(*sent.shape), out_specs=ANY, name="blank")()

    def of(count, pairs):
        def run(value):
            got = lax.ppermute(value[:count], axis, pairs)
            return got if count == full else lax.dynamic_update_slice(blank(), got, (0, 0, 0, 0))

        return run

    branches = [lambda value: blank()]
    branches += [of(count, pairs) for count in sizes for pairs in (ups + downs, ups, downs)[:kinds]]
    return lax.switch(branch, branches, sent)


def on_device(object_tiles, probe, prop_phase, amplitudes, offsets, counts):
    row = lax.axis_index("row").astype(I32)
    col = lax.axis_index("col").astype(I32)
    info = jnp.concatenate(
        [counts.reshape(1), offsets.reshape(8), jnp.stack([col % 2, row % 2, row, col]), jnp.zeros((3,), I32)]
    )
    near, far, meta = pl.pallas_call(
        pack_cols,
        out_shape=(shape(512, 128), shape(512, 128), shape(8, 128)),
        in_specs=[SMEM, VMEM],
        out_specs=(VMEM, VMEM, VMEM),
        compiler_params=PARAMS,
        name="pack_cols",
    )(info, object_tiles)
    far = lax.ppermute(far, "col", FAR_UP + FAR_DOWN)
    near = lax.ppermute(near, "col", NEAR_UP + NEAR_DOWN)
    meta_far = lax.ppermute(meta, "row", FAR_UP + FAR_DOWN)
    meta_near = lax.ppermute(meta, "row", NEAR_UP + NEAR_DOWN)
    line = lax.broadcasted_iota(I32, (8, 128), 0)
    odd = row % 2 == 1
    above = jnp.where(odd, meta_near, meta_far)
    below = jnp.where(odd, meta_far, meta_near)
    middle = jnp.where(line == 0, above, jnp.where(line == 1, meta, below))
    meta_far = lax.ppermute(middle, "col", FAR_UP + FAR_DOWN)
    meta_near = lax.ppermute(middle, "col", NEAR_UP + NEAR_DOWN)
    wide, own, s_near, s_far, tbl, b0, b1, b2, b3 = pl.pallas_call(
        plan,
        out_shape=(
            shape(4, TILE, 384),
            records(4),
            shape(12, 5, HALF, S),
            shape(12, 5, HALF, S),
            shape(T_SIZE, dtype=I32),
        )
        + (shape(1, dtype=I32),) * 4,
        in_specs=[SMEM] + [VMEM] * 7,
        out_specs=(VMEM, VMEM, VMEM, VMEM) + (SMEM,) * 5,
        scratch_shapes=[
            pltpu.VMEM((4, 512, 384), F32),
            pltpu.VMEM((24, 128), I32),
            pltpu.SMEM((24, 128), I32),
            pltpu.SMEM((16, 128), I32),
            pltpu.SemaphoreType.DMA((1,)),
        ],
        compiler_params=PARAMS,
        name="plan",
    )(info, object_tiles, near, far, middle, meta_near, meta_far, amplitudes)
    v_far = exchange(s_far, b1[0], "row", FAR_UP, FAR_DOWN, ROW_SIZES, 1)
    v_near = exchange(s_near, b0[0], "row", NEAR_UP, NEAR_DOWN, ROW_SIZES, 1)
    own, s_near, s_far = pl.pallas_call(
        merge,
        out_shape=(records(12), records(12), records(12)),
        in_specs=[SMEM, SMEM, ANY, VMEM, VMEM, VMEM],
        out_specs=(ANY, ANY, ANY),
        scratch_shapes=[
            pltpu.VMEM((4, 512, 384), F32),
            pltpu.VMEM((12, 5, S, S), F32),
            pltpu.SemaphoreType.DMA((36,)),
        ],
        compiler_params=PARAMS,
        name="merge",
    )(info, tbl, wide, own, v_near, v_far)
    h_far = exchange(s_far, b3[0], "col", FAR_UP, FAR_DOWN, COL_SIZES)
    h_near = exchange(s_near, b2[0], "col", NEAR_UP, NEAR_DOWN, CHIP_SIZES, 1)
    prop = jnp.stack([jnp.cos(prop_phase), jnp.sin(prop_phase)])
    return pl.pallas_call(
        sweeps,
        out_shape=shape(4, TILE, TILE),
        in_specs=[SMEM, VMEM, VMEM, VMEM, VMEM] + [ANY] * 3,
        out_specs=VMEM,
        scratch_shapes=[
            pltpu.VMEM((37, 5, S, S), F32),
            pltpu.VMEM((12, 776, 768), F32),
            pltpu.SemaphoreType.DMA((36,)),
        ],
        compiler_params=PARAMS,
        name="sweeps",
    )(tbl, object_tiles, probe, prop, jnp.asarray(wave_tables()), own, h_near, h_far)


def solution(mesh):
    return jax.shard_map(
        on_device,
        mesh=mesh,
        in_specs=(
            P(None, "row", "col"),
            P(),
            P(),
            P(None, "row", "col"),
            P("row", "col", None, None),
            P("row", "col"),
        ),
        out_specs=P(None, "row", "col"),
        check_vma=False,
    )
```

```python
import jax
import jax.numpy as jnp
import numpy as np
from jax import lax
from jax.experimental import pallas as pl
from jax.experimental.pallas import tpu as pltpu
from jax.sharding import PartitionSpec as P

S = 128
HALF = 64
TILE = 256
SLOTS = 4
LONG = S + 8
GROUP = 4
FAR = 1 << 20
LIMIT = 56 * 1024 * 1024
F32 = jnp.float32
I32 = jnp.int32

NEAR_UP = [(i, i + 1) for i in range(0, 16, 2)]
NEAR_DOWN = [(j, i) for i, j in NEAR_UP]
FAR_UP = [(i, i + 1) for i in range(1, 15, 2)]
FAR_DOWN = [(j, i) for i, j in FAR_UP]
ROW_SIZES = (2, 3, 4, 5, 6, 8, 12)
COL_SIZES = (1, 2, 3, 4, 5, 6, 8, 12)
CHIP_SIZES = (2, 4, 12)

T_N0 = 4
T_N1 = 5
T_NH = 6
T_ROW = 8
T_UNIT = 11
T_STEP = 20
T_NV = 10
T_PIECE = 12
T_COL = 24
T_CAME = 48
T_LIST1 = 80
T_MAIN = 128
T_SIZE = 384


def wave_tables():
    index = np.arange(S)
    phase = (index[:, None] * index[None, :] % S) * (2.0 * np.pi / S)
    cosine = np.cos(phase) / np.sqrt(S)
    sine = np.sin(phase) / np.sqrt(S)
    first = np.block([[cosine, sine], [-sine, cosine]])
    second = np.block([[cosine, -sine], [sine, cosine]])
    return np.stack([first, second]).astype(jnp.bfloat16)


def roll(x, by):
    return pltpu.roll(x, by, 1)


def pack_cols(info, tile, near, far, meta):
    lane = lax.broadcasted_iota(I32, (TILE, 128), 1)
    low = lane < HALF
    odd = (lane * 0 + info[9]) == 1
    for q in range(2):
        a0, a1 = tile[2 * q, :, 0:128], tile[2 * q, :, 128:256]
        b0, b1 = tile[2 * q + 1, :, 0:128], tile[2 * q + 1, :, 128:256]
        left = jnp.where(low, a0, roll(b0, HALF))
        right = jnp.where(low, roll(a1, HALF), b1)
        rows = slice(q * TILE, (q + 1) * TILE)
        near[rows, :] = jnp.where(odd, left, right)
        far[rows, :] = jnp.where(odd, right, left)
    lane = lax.broadcasted_iota(I32, (8, 128), 1)
    mine = jnp.zeros((8, 128), I32)
    for k in range(9):
        mine = jnp.where(lane == k, info[k], mine)
    meta[...] = mine.astype(F32)


def tile_touch(r, c, row0, col0):
    return (r < row0 + TILE) & (r + S > row0) & (c < col0 + TILE) & (c + S > col0)


def pick(ref, lead, r, c, lane):
    line = pl.multiple_of((r // 8) * 8, 8)
    block = pl.multiple_of((c // 128) * 128, 128)
    rest = c % 128
    step = r % 8
    back = (128 - rest) % 128
    one = roll(ref[lead, pl.ds(line, LONG), pl.ds(block, 128)], back)
    two = roll(ref[lead, pl.ds(line, LONG), pl.ds(block + 128, 128)], back)
    wide = jnp.where(lane < 128 - rest, one, two).reshape(LONG // 8, 8, 128)
    wide = pltpu.roll(wide, (8 - step) % 8, 1)
    sub = lax.broadcasted_iota(I32, (S // 8, 8, 128), 1)
    return jnp.where(sub < 8 - step, wide[:-1], wide[1:]).reshape(S, 128)


def put(ref, lead, r, c, value, lane):
    line = pl.multiple_of((r // 8) * 8, 8)
    block = pl.multiple_of((c // 128) * 128, 128)
    rest = c % 128
    step = r % 8
    moved = pltpu.roll(roll(value, rest).reshape(S // 8, 8, 128), step, 1)
    sub = lax.broadcasted_iota(I32, (LONG // 8, 8, 128), 1)
    none = jnp.zeros((1, 8, 128), F32)
    moved = jnp.where(sub >= step, jnp.concatenate([moved, none]), jnp.concatenate([none, moved])).reshape(LONG, 128)
    zero = jnp.zeros_like(moved)
    ref[lead, pl.ds(line, LONG), pl.ds(block, 128)] += jnp.where(lane >= rest, moved, zero)
    ref[lead, pl.ds(line, LONG), pl.ds(block + 128, 128)] += jnp.where(lane < rest, moved, zero)


def step_of(most, sizes):
    step = jnp.int32(1)
    for size in sizes[:-1]:
        step = step + jnp.where(most > size, 1, 0)
    return jnp.where(most == 0, 0, step)


def branch_of(step, sent, got, lower):
    up = jnp.where(lower, sent, got)
    down = jnp.where(lower, got, sent)
    kind = jnp.where(down == 0, 1, jnp.where(up == 0, 2, 0))
    return jnp.where(step == 0, 0, 3 * step - 2 + kind)


def plan(info, tile, near, far, middle, meta_near, meta_far, amps, wide, own, *rest):
    kinds = len(ROW_SIZES)
    to_near, to_far = rest[:kinds], rest[kinds : 2 * kinds]
    tbl, b0, b1, b2, b3, ext, s_near, s_far, vec, meta_s, need_s, sems = rest[2 * kinds :]
    lane8 = lax.broadcasted_iota(I32, (8, 128), 1)
    odd8 = (lane8 * 0 + info[9]) == 1
    vec[0:8, :] = jnp.where(odd8, meta_near[...], meta_far[...]).astype(I32)
    vec[8:16, :] = middle[...].astype(I32)
    vec[16:24, :] = jnp.where(odd8, meta_far[...], meta_near[...]).astype(I32)
    copy = pltpu.make_async_copy(vec, meta_s, sems.at[0])
    copy.start()

    lane = lax.broadcasted_iota(I32, (TILE, 128), 1)
    low = lane < HALF
    odd = (lane * 0 + info[9]) == 1
    for q in range(2):
        rows = slice(q * TILE, (q + 1) * TILE)
        left = jnp.where(odd, near[rows, :], far[rows, :])
        right = jnp.where(odd, far[rows, :], near[rows, :])
        for k in range(2):
            p = 2 * q + k
            t0, t1 = roll(tile[p, :, 0:128], HALF), roll(tile[p, :, 128:256], HALF)
            lft = left if k == 0 else roll(left, HALF)
            rgt = roll(right, HALF) if k == 0 else right
            parts = (jnp.where(low, lft, t0), jnp.where(low, t0, t1), jnp.where(low, t1, rgt))
            for b in range(3):
                wide[p, :, b * 128 : (b + 1) * 128] = parts[b]
                ext[p, S : S + TILE, b * 128 : (b + 1) * 128] = parts[b]
    copy.wait()

    def spot(j):
        t, s = j // SLOTS, j % SLOTS
        at = (t % 3) * 8 + t // 3
        return (
            meta_s[at, 1 + 2 * s] + (t // 3 - 1) * TILE,
            meta_s[at, 2 + 2 * s] + (t % 3 - 1) * TILE,
            jnp.where(s < meta_s[at, 0], 1, 0),
        )

    lane = lax.broadcasted_iota(I32, (16, 128), 1)
    tile_row = lax.broadcasted_iota(I32, (16, 128), 0)
    row0 = (tile_row // 3 - 1) * TILE
    col0 = (tile_row % 3 - 1) * TILE
    rows_v = jnp.full((16, 128), FAR, I32)
    cols_v = jnp.full((16, 128), FAR, I32)
    where_r, where_c = [], []
    for j in range(36):
        r, c, used = spot(j)
        r = jnp.where(used == 1, r, FAR)
        where_r.append(r)
        where_c.append(c)
        rows_v = jnp.where(lane == j, r, rows_v)
        cols_v = jnp.where(lane == j, c, cols_v)
    need = tile_touch(rows_v, cols_v, row0, col0)
    for j in range(36):
        r, c = where_r[j], where_c[j]
        over = (rows_v - r < S) & (r - rows_v < S) & (cols_v - c < S) & (c - cols_v < S)
        need = need | (tile_touch(r, c, row0, col0) & over)
    there_row = tile_row // 3 - 1 + info[11]
    there_col = tile_row % 3 - 1 + info[12]
    inside = (there_row >= 0) & (there_row < 16) & (there_col >= 0) & (there_col < 16)
    vec[0:16, :] = jnp.where(need & inside & (rows_v < FAR), 1, 0)
    copy = pltpu.make_async_copy(vec.at[0:16], need_s, sems.at[0])
    copy.start()
    lane_s = lax.broadcasted_iota(I32, (LONG, S), 1)

    @pl.loop(0, info[0])
    def _(s):
        r = info[1 + 2 * s] + S
        c = info[2 + 2 * s] + HALF
        for p in range(4):
            own[s, p] = pick(ext, p, r, c, lane_s)
        own[s, 4] = amps[s]

    copy.wait()

    side_near = 1 - 2 * info[9]
    row_near = 1 - 2 * info[10]
    for k in (T_N0, T_N1, T_NH, T_NH + 1, T_NV):
        tbl[k] = 0
    tbl[T_ROW] = info[11] * TILE
    tbl[T_ROW + 1] = info[12] * TILE

    def add_main(buf, pos, r, c):
        n0 = tbl[T_N0]
        tbl[T_MAIN + 4 * n0] = buf
        tbl[T_MAIN + 4 * n0 + 1] = pos
        tbl[T_MAIN + 4 * n0 + 2] = r
        tbl[T_MAIN + 4 * n0 + 3] = c
        tbl[T_N0] = n0 + 1

        @pl.when(tile_touch(r, c, 0, 0))
        def _():
            n1 = tbl[T_N1]
            tbl[T_LIST1 + n1] = n0
            tbl[T_N1] = n1 + 1

    def add_send(j, slot):
        for e, side in enumerate((side_near, -side_near)):

            @pl.when(need_s[4 + side, j] == 1)
            def _():
                n = tbl[T_NH + e]
                tbl[T_COL + 12 * e + n] = slot
                tbl[T_NH + e] = n + 1

    def wanted(j, up):
        t = 4 + 3 * up
        return need_s[t - 1, j] | need_s[t, j] | need_s[t + 1, j]

    sent = []
    for up, buf in ((row_near, s_near), (-row_near, s_far)):
        count = jnp.int32(0)
        for s in range(SLOTS):
            flag = wanted(16 + s, up)

            @pl.when(flag == 1)
            def _():
                for p in range(5):
                    buf[count, p] = own[s, p, 0:HALF, :]
                    buf[count + 1, p] = own[s, p, HALF:S, :]

            count = count + 2 * flag
        tbl[T_UNIT] = count

        @pl.loop(0, meta_s[9 + up, 0])
        def _(s):
            r = meta_s[9 + up, 1 + 2 * s] + up * TILE
            c = meta_s[9 + up, 2 + 2 * s]

            @pl.when((r < TILE) & (r + S > 0))
            def _():
                count = tbl[T_UNIT]
                for p in range(4):
                    got = pick(ext, p, r + S, c + HALF, lane_s)
                    buf[count, p] = jnp.where(up == 1, got[0:HALF], got[HALF:S])
                tbl[T_UNIT] = count + 1

        sent.append(tbl[T_UNIT])
    for s in range(SLOTS):

        @pl.when(s < info[0])
        def _():
            add_main(0, s, info[1 + 2 * s], info[2 + 2 * s])
            add_send(16 + s, s)

    got = []
    for up in (-1, 1):
        buf = jnp.where(row_near == up, 0, 1)
        count = jnp.int32(0)
        for s in range(SLOTS):
            j = (4 + 3 * up) * SLOTS + s
            flag = need_s[3, j] | need_s[4, j] | need_s[5, j]

            @pl.when(flag == 1)
            def _():
                r, c, _ = spot(j)
                n = tbl[T_NV]
                tbl[T_CAME + 4 * n] = buf
                tbl[T_CAME + 4 * n + 1] = count
                tbl[T_CAME + 4 * n + 2] = r
                tbl[T_CAME + 4 * n + 3] = c
                tbl[T_NV] = n + 1

                @pl.when(need_s[4, j] == 1)
                def _():
                    add_main(0, SLOTS + n, r, c)

                add_send(j, SLOTS + n)

            count = count + 2 * flag
        for s in range(SLOTS):
            r = info[1 + 2 * s]
            out = (r < 0) if up == -1 else (r + S > TILE)
            there = info[11] + up
            flag = jnp.where((s < info[0]) & out & (there >= 0) & (there < 16), 1, 0)
            tbl[T_PIECE + 2 * s + (up + 1) // 2] = jnp.where(flag == 1, count, -1)
            count = count + flag
        got.append(count)
    got_near = jnp.where(row_near == 1, got[1], got[0])
    got_far = jnp.where(row_near == 1, got[0], got[1])
    for e, (number, most) in enumerate(
        ((b0, jnp.maximum(sent[0], got_near)), (b1, jnp.maximum(sent[1], got_far)))
    ):
        step = step_of(most, ROW_SIZES)
        number[0] = step
        tbl[T_STEP + e] = step

    def ship(act):
        for e, (source, targets) in enumerate(((s_near, to_near), (s_far, to_far))):
            for k, size in enumerate(ROW_SIZES):

                @pl.when(tbl[T_STEP + e] == k + 1)
                def _():
                    act(pltpu.make_async_copy(source.at[0:size], targets[k], sems.at[1 + e]))

    ship(lambda copy: copy.start())

    got = []
    for side in (-1, 1):
        buf = jnp.where(side_near == side, 1, 2)
        count = jnp.int32(0)
        for t in (4 + side, 1 + side, 7 + side):
            for s in range(SLOTS):
                j = t * SLOTS + s
                flag = need_s[4, j]

                @pl.when(flag == 1)
                def _():
                    r, c, _ = spot(j)
                    add_main(buf, count, r, c)

                count = count + flag
        got.append(count)
    got_near = jnp.where(side_near == 1, got[1], got[0])
    got_far = jnp.where(side_near == 1, got[0], got[1])
    step = step_of(jnp.maximum(tbl[T_NH], got_near), CHIP_SIZES)
    tbl[T_STEP + 2] = step
    b2[0] = step
    step = step_of(jnp.maximum(tbl[T_NH + 1], got_far), COL_SIZES)
    tbl[T_STEP + 3] = step
    b3[0] = branch_of(step, tbl[T_NH + 1], got_far, info[9] == 1)
    ship(lambda copy: copy.wait())


def merge(info, tbl, wide, own, *rest):
    rows, chips, cols = len(ROW_SIZES), len(CHIP_SIZES), len(COL_SIZES)
    came = (rest[:rows], rest[rows : 2 * rows])
    out, rest = rest[2 * rows], rest[2 * rows + 1 :]
    targets = (rest[:chips], rest[chips : chips + cols])
    ext, rec, vbuf, sems = rest[chips + cols :]

    def fetch(act):
        for e in range(2):
            for k, size in enumerate(ROW_SIZES):

                @pl.when(tbl[T_STEP + e] == k + 1)
                def _():
                    act(pltpu.make_async_copy(came[e][k], vbuf.at[e, 0:size], sems.at[1 + e]))

    fetch(lambda copy: copy.start())
    copy = pltpu.make_async_copy(wide, ext.at[:, S : S + TILE], sems.at[0])
    copy.start()
    fetch(lambda copy: copy.wait())
    high = lax.broadcasted_iota(I32, (S, S), 0)
    lane = lax.broadcasted_iota(I32, (LONG, S), 1)

    def half(far, unit, p):
        return vbuf[far, unit, p]

    for s in range(SLOTS):

        @pl.when(s < info[0])
        def _():
            for p in range(5):
                rec[s, p] = own[s, p]
            r = info[1 + 2 * s]
            above, below = tbl[T_PIECE + 2 * s], tbl[T_PIECE + 2 * s + 1]
            top = high[0:HALF] + r < 0
            bottom = high[HALF:S] + r >= TILE
            zero = jnp.zeros((HALF, S), F32)

            @pl.when(r < 0)
            def _():
                for p in range(4):
                    part = jnp.where(above >= 0, half(1 - info[10], jnp.maximum(above, 0), p), zero)
                    rec[s, p, 0:HALF] = jnp.where(top, part, rec[s, p, 0:HALF])

            @pl.when(r + S > TILE)
            def _():
                for p in range(4):
                    part = jnp.where(below >= 0, half(info[10], jnp.maximum(below, 0), p), zero)
                    rec[s, p, HALF:S] = jnp.where(bottom, part, rec[s, p, HALF:S])

    copy.wait()

    @pl.loop(0, tbl[T_NV])
    def _(i):
        far = tbl[T_CAME + 4 * i]
        unit = tbl[T_CAME + 4 * i + 1]
        r = tbl[T_CAME + 4 * i + 2]
        c = tbl[T_CAME + 4 * i + 3]
        slot = SLOTS + i
        for p in range(5):
            rec[slot, p, 0:HALF] = half(far, unit, p)
            rec[slot, p, HALF:S] = half(far, unit + 1, p)

        @pl.when((r < TILE) & (r + S > 0))
        def _():
            mine = (high + r >= 0) & (high + r < TILE)
            for p in range(4):
                rec[slot, p] = jnp.where(mine, pick(ext, p, r + S, c + HALF, lane), rec[slot, p])

    many = tbl[T_NV]

    def keep(k):
        return pltpu.make_async_copy(rec.at[k], out.at[k], sems.at[k])

    for e in range(2):

        @pl.loop(0, tbl[T_NH + e])
        def _(i):
            for k, target in enumerate(targets[e]):

                @pl.when(tbl[T_STEP + 2 + e] == k + 1)
                def _():
                    source = rec.at[tbl[T_COL + 12 * e + i]]
                    pltpu.make_async_copy(source, target.at[i], sems.at[12 + 12 * e + i]).start()

    @pl.loop(0, info[0])
    def _(i):
        keep(i).start()

    @pl.loop(SLOTS, SLOTS + many)
    def _(i):
        keep(i).start()

    for e in range(2):

        @pl.loop(0, tbl[T_NH + e])
        def _(i):
            pltpu.make_async_copy(rec.at[0], out.at[0], sems.at[12 + 12 * e + i]).wait()

    @pl.loop(0, info[0])
    def _(i):
        keep(i).wait()

    @pl.loop(SLOTS, SLOTS + many)
    def _(i):
        keep(i).wait()


def times(a, b):
    return (a[0] * b[0] - a[1] * b[1], a[0] * b[1] + a[1] * b[0])


def conj_times(a, b):
    return (a[0] * b[0] + a[1] * b[1], a[0] * b[1] - a[1] * b[0])


def transform(x, left, right):
    return [y for k in range(0, GROUP, 2) for y in transform_pair(x[k : k + 2], left, right)]


def transform_pair(x, left, right):
    half = [jnp.concatenate([w[k].astype(jnp.bfloat16) for w in x], axis=1) for k in range(2)]
    half = jnp.concatenate(half, axis=0)
    half = jnp.dot(left, half, preferred_element_type=F32).astype(jnp.bfloat16)
    half = [jnp.concatenate([half[:S, at], half[S:, at]], axis=1) for at in (slice(0, S), slice(S, 2 * S))]
    done = jnp.dot(jnp.concatenate(half, axis=0), right, preferred_element_type=F32)
    return [(done[at, :S], done[at, S:]) for at in (slice(0, S), slice(S, 2 * S))]


def sweeps(tbl, tile, probe, prop, waves, own, *rest):
    chips, cols = len(CHIP_SIZES), len(COL_SIZES)
    out, rec, acc, sems = rest[chips + cols :]
    sources = [(0, None, own)]
    sources += [(1, k + 1, source) for k, source in enumerate(rest[:chips])]
    sources += [(2, k + 1, source) for k, source in enumerate(rest[chips : chips + cols])]
    n0 = tbl[T_N0]
    n1 = tbl[T_N1]

    @pl.loop(0, n0)
    def _(i):
        buf = tbl[T_MAIN + 4 * i]
        pos = tbl[T_MAIN + 4 * i + 1]
        for b, step, source in sources:

            @pl.when((buf == b) if step is None else ((buf == b) & (tbl[T_STEP + 1 + b] == step)))
            def _():
                pltpu.make_async_copy(source.at[pos], rec.at[i], sems.at[i]).start()

    @pl.loop(0, 12)
    def _(p):
        acc[p, 256:512, 256:512] = jnp.zeros((256, 256), F32)

        @pl.when(p < 6)
        def _():
            acc[p, 128:256, 128:640] = jnp.zeros((128, 512), F32)
            acc[p, 512:640, 128:640] = jnp.zeros((128, 512), F32)
            acc[p, 256:512, 128:256] = jnp.zeros((256, 128), F32)
            acc[p, 256:512, 512:640] = jnp.zeros((256, 128), F32)

    lane = lax.broadcasted_iota(I32, (LONG, S), 1)
    def group(i, base, count, second):
        at = []
        for k in range(GROUP):
            place = GROUP * i + k
            there = place < count
            e = tbl[T_LIST1 + jnp.minimum(place, 35)] if second else place
            e = jnp.where(there, e, 36)
            r = jnp.where(there, tbl[T_MAIN + 4 * e + 2] + TILE, 5 * S)
            c = jnp.where(there, tbl[T_MAIN + 4 * e + 3] + TILE, 0)
            at.append((e, r, c))
            if second:
                high = tbl[T_ROW] + r - TILE + lax.broadcasted_iota(I32, (S, S), 0)
                wide = tbl[T_ROW + 1] + c - TILE + lax.broadcasted_iota(I32, (S, S), 1)
                inside = (high >= 0) & (high < 16 * TILE) & (wide >= 0) & (wide < 16 * TILE)
                for m in range(2):
                    scale = jnp.where(inside, 1.0 / (pick(acc, 4 + m, r, c, lane) + 1.0), 0.0)
                    for p in (2 * m, 2 * m + 1):
                        rec[e, p] = rec[e, p] - pick(acc, p, r, c, lane) * scale
            else:

                @pl.when(there)
                def _():
                    pltpu.make_async_copy(own.at[0], rec.at[e], sems.at[e]).wait()

        wave = (probe[0], probe[1])
        spread = (prop[0], prop[1])
        one, two = waves[0], waves[1]
        exits = [times(wave, (rec[e, 0], rec[e, 1])) for e, _, _ in at]
        inner = transform([times(spread, x) for x in transform(exits, one, two)], two, one)
        o2 = [(rec[e, 2], rec[e, 3]) for e, _, _ in at]
        field = transform([times(x, o) for x, o in zip(inner, o2)], one, two)
        chi = []
        for (e, _, _), f in zip(at, field):
            size = jnp.sqrt(f[0] * f[0] + f[1] * f[1])
            keep = 1.0 - rec[e, 4] / jnp.maximum(size, 1.0)
            chi.append((f[0] * keep, f[1] * keep))
        g2 = transform(chi, two, one)
        for (_, r, c), x, g in zip(at, inner, g2):
            later = conj_times(x, g)
            put(acc, base + 2, r, c, later[0], lane)
            put(acc, base + 3, r, c, later[1], lane)
            put(acc, base + 5, r, c, x[0] * x[0] + x[1] * x[1], lane)
        back = transform([conj_times(o, g) for o, g in zip(o2, g2)], one, two)
        first = transform([conj_times(spread, x) for x in back], two, one)
        light = wave[0] * wave[0] + wave[1] * wave[1]
        for (_, r, c), g in zip(at, first):
            low = conj_times(wave, g)
            put(acc, base, r, c, low[0], lane)
            put(acc, base + 1, r, c, low[1], lane)
            put(acc, base + 4, r, c, light, lane)

    @pl.loop(0, (n0 + GROUP - 1) // GROUP)
    def _(i):
        group(i, 0, n0, False)

    @pl.loop(0, (n1 + GROUP - 1) // GROUP)
    def _(i):
        group(i, 6, n1, True)

    for k in range(2):
        one = 1.0 / (acc[4 + k, 256:512, 256:512] + 1.0)
        two = 1.0 / (acc[10 + k, 256:512, 256:512] + 1.0)
        for p in (2 * k, 2 * k + 1):
            out[p] = tile[p] - acc[p, 256:512, 256:512] * one - acc[6 + p, 256:512, 256:512] * two


VMEM = pl.BlockSpec(memory_space=pltpu.VMEM)
SMEM = pl.BlockSpec(memory_space=pltpu.SMEM)
ANY = pl.BlockSpec(memory_space=pl.ANY)
PARAMS = pltpu.CompilerParams(vmem_limit_bytes=LIMIT)


def shape(*dims, dtype=F32):
    return jax.ShapeDtypeStruct(dims, dtype)


def records(count):
    return shape(count, 5, S, S)


def nothing(out):
    pass


def exchange(sent, branch, axis, ups, downs, kinds):
    def blank(like):
        return pl.pallas_call(nothing, out_shape=shape(*like.shape), out_specs=ANY, name="blank")()

    def of(k, pairs):
        def run(*values):
            got = [blank(value) for value in values]
            if pairs:
                got[k] = lax.ppermute(values[k], axis, pairs)
            return tuple(got)

        return run

    branches = [of(0, None)]
    branches += [of(k, pairs) for k in range(len(sent)) for pairs in (ups + downs, ups, downs)[:kinds]]
    return lax.switch(branch, branches, *sent)


def on_device(object_tiles, probe, prop_phase, amplitudes, offsets, counts):
    row = lax.axis_index("row").astype(I32)
    col = lax.axis_index("col").astype(I32)
    info = jnp.concatenate(
        [counts.reshape(1), offsets.reshape(8), jnp.stack([col % 2, row % 2, row, col]), jnp.zeros((3,), I32)]
    )
    near, far, meta = pl.pallas_call(
        pack_cols,
        out_shape=(shape(512, 128), shape(512, 128), shape(8, 128)),
        in_specs=[SMEM, VMEM],
        out_specs=(VMEM, VMEM, VMEM),
        compiler_params=PARAMS,
        name="pack_cols",
    )(info, object_tiles)
    far = lax.ppermute(far, "col", FAR_UP + FAR_DOWN)
    near = lax.ppermute(near, "col", NEAR_UP + NEAR_DOWN)
    meta_far = lax.ppermute(meta, "row", FAR_UP + FAR_DOWN)
    meta_near = lax.ppermute(meta, "row", NEAR_UP + NEAR_DOWN)
    line = lax.broadcasted_iota(I32, (8, 128), 0)
    odd = row % 2 == 1
    above = jnp.where(odd, meta_near, meta_far)
    below = jnp.where(odd, meta_far, meta_near)
    middle = jnp.where(line == 0, above, jnp.where(line == 1, meta, below))
    meta_far = lax.ppermute(middle, "col", FAR_UP + FAR_DOWN)
    meta_near = lax.ppermute(middle, "col", NEAR_UP + NEAR_DOWN)
    halves = tuple(shape(size, 5, HALF, S) for size in ROW_SIZES)
    rows, chips, cols = len(ROW_SIZES), len(CHIP_SIZES), len(COL_SIZES)
    wide, own, *made = pl.pallas_call(
        plan,
        out_shape=(shape(4, TILE, 384), records(4))
        + halves
        + halves
        + (shape(T_SIZE, dtype=I32),)
        + (shape(1, dtype=I32),) * 4,
        in_specs=[SMEM] + [VMEM] * 7,
        out_specs=(VMEM, VMEM) + (ANY,) * (2 * rows) + (SMEM,) * 5,
        scratch_shapes=[
            pltpu.VMEM((4, 512, 384), F32),
            pltpu.VMEM((12, 5, HALF, S), F32),
            pltpu.VMEM((12, 5, HALF, S), F32),
            pltpu.VMEM((24, 128), I32),
            pltpu.SMEM((24, 128), I32),
            pltpu.SMEM((16, 128), I32),
            pltpu.SemaphoreType.DMA((3,)),
        ],
        compiler_params=PARAMS,
        name="plan",
    )(info, object_tiles, near, far, middle, meta_near, meta_far, amplitudes)
    tbl, b0, b1, b2, b3 = made[2 * rows :]
    v_far = exchange(made[rows : 2 * rows], b1[0], "row", FAR_UP, FAR_DOWN, 1)
    v_near = exchange(made[:rows], b0[0], "row", NEAR_UP, NEAR_DOWN, 1)
    own, *made = pl.pallas_call(
        merge,
        out_shape=(records(12),) + tuple(records(size) for size in CHIP_SIZES + COL_SIZES),
        in_specs=[SMEM, SMEM, ANY, VMEM] + [ANY] * (2 * rows),
        out_specs=(ANY,) * (1 + chips + cols),
        scratch_shapes=[
            pltpu.VMEM((4, 512, 384), F32),
            pltpu.VMEM((12, 5, S, S), F32),
            pltpu.VMEM((2, 12, 5, HALF, S), F32),
            pltpu.SemaphoreType.DMA((36,)),
        ],
        compiler_params=PARAMS,
        name="merge",
    )(info, tbl, wide, own, *v_near, *v_far)
    h_far = exchange(made[chips:], b3[0], "col", FAR_UP, FAR_DOWN, 3)
    h_near = exchange(made[:chips], b2[0], "col", NEAR_UP, NEAR_DOWN, 1)
    prop = jnp.stack([jnp.cos(prop_phase), jnp.sin(prop_phase)])
    return pl.pallas_call(
        sweeps,
        out_shape=shape(4, TILE, TILE),
        in_specs=[SMEM, VMEM, VMEM, VMEM, VMEM] + [ANY] * (1 + chips + cols),
        out_specs=VMEM,
        scratch_shapes=[
            pltpu.VMEM((37, 5, S, S), F32),
            pltpu.VMEM((12, 776, 768), F32),
            pltpu.SemaphoreType.DMA((36,)),
        ],
        compiler_params=PARAMS,
        name="sweeps",
    )(tbl, object_tiles, probe, prop, jnp.asarray(wave_tables()), own, *h_near, *h_far)


def solution(mesh):
    return jax.shard_map(
        on_device,
        mesh=mesh,
        in_specs=(
            P(None, "row", "col"),
            P(),
            P(),
            P(None, "row", "col"),
            P("row", "col", None, None),
            P("row", "col"),
        ),
        out_specs=P(None, "row", "col"),
        check_vma=False,
    )
```

```python
import jax
import jax.numpy as jnp
import numpy as np
from jax import lax
from jax.experimental import pallas as pl
from jax.experimental.pallas import tpu as pltpu
from jax.sharding import PartitionSpec as P

S = 128
HALF = 64
TILE = 256
SLOTS = 4
LONG = S + 8
GROUP = 4
FAR = 1 << 20
LIMIT = 56 * 1024 * 1024
F32 = jnp.float32
I32 = jnp.int32

NEAR_UP = [(i, i + 1) for i in range(0, 16, 2)]
NEAR_DOWN = [(j, i) for i, j in NEAR_UP]
FAR_UP = [(i, i + 1) for i in range(1, 15, 2)]
FAR_DOWN = [(j, i) for i, j in FAR_UP]
ROW_SIZES = (2, 3, 4, 5, 6, 7, 8, 10, 12)
COL_SIZES = (1, 2, 3, 4, 5, 6, 7, 8, 10, 12)
CHIP_SIZES = (2, 4, 12)

T_N0 = 4
T_N1 = 5
T_NH = 6
T_ROW = 8
T_UNIT = 11
T_STEP = 20
T_NV = 10
T_PIECE = 12
T_COL = 24
T_CAME = 48
T_LIST1 = 80
T_MAIN = 128
T_SIZE = 384


def wave_tables():
    index = np.arange(S)
    phase = (index[:, None] * index[None, :] % S) * (2.0 * np.pi / S)
    cosine = np.cos(phase) / np.sqrt(S)
    sine = np.sin(phase) / np.sqrt(S)
    first = np.block([[cosine, sine], [-sine, cosine]])
    second = np.block([[cosine, -sine], [sine, cosine]])
    return np.stack([first, second]).astype(jnp.bfloat16)


def roll(x, by):
    return pltpu.roll(x, by, 1)


def pack_cols(info, tile, near, far, meta):
    lane = lax.broadcasted_iota(I32, (TILE, 128), 1)
    low = lane < HALF
    odd = (lane * 0 + info[9]) == 1
    for q in range(2):
        a0, a1 = tile[2 * q, :, 0:128], tile[2 * q, :, 128:256]
        b0, b1 = tile[2 * q + 1, :, 0:128], tile[2 * q + 1, :, 128:256]
        left = jnp.where(low, a0, roll(b0, HALF))
        right = jnp.where(low, roll(a1, HALF), b1)
        rows = slice(q * TILE, (q + 1) * TILE)
        near[rows, :] = jnp.where(odd, left, right)
        far[rows, :] = jnp.where(odd, right, left)
    lane = lax.broadcasted_iota(I32, (8, 128), 1)
    mine = jnp.zeros((8, 128), I32)
    for k in range(9):
        mine = jnp.where(lane == k, info[k], mine)
    meta[...] = mine.astype(F32)


def tile_touch(r, c, row0, col0):
    return (r < row0 + TILE) & (r + S > row0) & (c < col0 + TILE) & (c + S > col0)


def pick(ref, lead, r, c, lane):
    line = pl.multiple_of((r // 8) * 8, 8)
    block = pl.multiple_of((c // 128) * 128, 128)
    rest = c % 128
    step = r % 8
    back = (128 - rest) % 128
    one = roll(ref[lead, pl.ds(line, LONG), pl.ds(block, 128)], back)
    two = roll(ref[lead, pl.ds(line, LONG), pl.ds(block + 128, 128)], back)
    wide = jnp.where(lane < 128 - rest, one, two).reshape(LONG // 8, 8, 128)
    wide = pltpu.roll(wide, (8 - step) % 8, 1)
    sub = lax.broadcasted_iota(I32, (S // 8, 8, 128), 1)
    return jnp.where(sub < 8 - step, wide[:-1], wide[1:]).reshape(S, 128)


def put(ref, lead, r, c, value, lane):
    line = pl.multiple_of((r // 8) * 8, 8)
    block = pl.multiple_of((c // 128) * 128, 128)
    rest = c % 128
    step = r % 8
    moved = pltpu.roll(roll(value, rest).reshape(S // 8, 8, 128), step, 1)
    sub = lax.broadcasted_iota(I32, (LONG // 8, 8, 128), 1)
    none = jnp.zeros((1, 8, 128), F32)
    moved = jnp.where(sub >= step, jnp.concatenate([moved, none]), jnp.concatenate([none, moved])).reshape(LONG, 128)
    zero = jnp.zeros_like(moved)
    ref[lead, pl.ds(line, LONG), pl.ds(block, 128)] += jnp.where(lane >= rest, moved, zero)
    ref[lead, pl.ds(line, LONG), pl.ds(block + 128, 128)] += jnp.where(lane < rest, moved, zero)


def step_of(most, sizes):
    step = jnp.int32(1)
    for size in sizes[:-1]:
        step = step + jnp.where(most > size, 1, 0)
    return jnp.where(most == 0, 0, step)


def branch_of(step, sent, got, lower):
    up = jnp.where(lower, sent, got)
    down = jnp.where(lower, got, sent)
    kind = jnp.where(down == 0, 1, jnp.where(up == 0, 2, 0))
    return jnp.where(step == 0, 0, 3 * step - 2 + kind)


def plan(info, tile, near, far, middle, meta_near, meta_far, amps, wide, own, *rest):
    kinds = len(ROW_SIZES)
    to_near, to_far = rest[:kinds], rest[kinds : 2 * kinds]
    tbl, b0, b1, b2, b3, ext, s_near, s_far, vec, meta_s, need_s, sems = rest[2 * kinds :]
    lane8 = lax.broadcasted_iota(I32, (8, 128), 1)
    odd8 = (lane8 * 0 + info[9]) == 1
    vec[0:8, :] = jnp.where(odd8, meta_near[...], meta_far[...]).astype(I32)
    vec[8:16, :] = middle[...].astype(I32)
    vec[16:24, :] = jnp.where(odd8, meta_far[...], meta_near[...]).astype(I32)
    copy = pltpu.make_async_copy(vec, meta_s, sems.at[0])
    copy.start()

    lane = lax.broadcasted_iota(I32, (TILE, 128), 1)
    low = lane < HALF
    odd = (lane * 0 + info[9]) == 1
    for q in range(2):
        rows = slice(q * TILE, (q + 1) * TILE)
        left = jnp.where(odd, near[rows, :], far[rows, :])
        right = jnp.where(odd, far[rows, :], near[rows, :])
        for k in range(2):
            p = 2 * q + k
            t0, t1 = roll(tile[p, :, 0:128], HALF), roll(tile[p, :, 128:256], HALF)
            lft = left if k == 0 else roll(left, HALF)
            rgt = roll(right, HALF) if k == 0 else right
            parts = (jnp.where(low, lft, t0), jnp.where(low, t0, t1), jnp.where(low, t1, rgt))
            for b in range(3):
                wide[p, :, b * 128 : (b + 1) * 128] = parts[b]
                ext[p, S : S + TILE, b * 128 : (b + 1) * 128] = parts[b]
    copy.wait()

    def spot(j):
        t, s = j // SLOTS, j % SLOTS
        at = (t % 3) * 8 + t // 3
        return (
            meta_s[at, 1 + 2 * s] + (t // 3 - 1) * TILE,
            meta_s[at, 2 + 2 * s] + (t % 3 - 1) * TILE,
            jnp.where(s < meta_s[at, 0], 1, 0),
        )

    lane = lax.broadcasted_iota(I32, (16, 128), 1)
    tile_row = lax.broadcasted_iota(I32, (16, 128), 0)
    row0 = (tile_row // 3 - 1) * TILE
    col0 = (tile_row % 3 - 1) * TILE
    rows_v = jnp.full((16, 128), FAR, I32)
    cols_v = jnp.full((16, 128), FAR, I32)
    where_r, where_c = [], []
    for j in range(36):
        r, c, used = spot(j)
        r = jnp.where(used == 1, r, FAR)
        where_r.append(r)
        where_c.append(c)
        rows_v = jnp.where(lane == j, r, rows_v)
        cols_v = jnp.where(lane == j, c, cols_v)
    need = tile_touch(rows_v, cols_v, row0, col0)
    for j in range(36):
        r, c = where_r[j], where_c[j]
        over = (rows_v - r < S) & (r - rows_v < S) & (cols_v - c < S) & (c - cols_v < S)
        need = need | (tile_touch(r, c, row0, col0) & over)
    there_row = tile_row // 3 - 1 + info[11]
    there_col = tile_row % 3 - 1 + info[12]
    inside = (there_row >= 0) & (there_row < 16) & (there_col >= 0) & (there_col < 16)
    vec[0:16, :] = jnp.where(need & inside & (rows_v < FAR), 1, 0)
    copy = pltpu.make_async_copy(vec.at[0:16], need_s, sems.at[0])
    copy.start()
    lane_s = lax.broadcasted_iota(I32, (LONG, S), 1)

    @pl.loop(0, info[0])
    def _(s):
        r = info[1 + 2 * s] + S
        c = info[2 + 2 * s] + HALF
        for p in range(4):
            own[s, p] = pick(ext, p, r, c, lane_s)
        own[s, 4] = amps[s]

    copy.wait()

    side_near = 1 - 2 * info[9]
    row_near = 1 - 2 * info[10]
    for k in (T_N0, T_N1, T_NH, T_NH + 1, T_NV):
        tbl[k] = 0
    tbl[T_ROW] = info[11] * TILE
    tbl[T_ROW + 1] = info[12] * TILE

    def add_main(buf, pos, r, c):
        n0 = tbl[T_N0]
        tbl[T_MAIN + 4 * n0] = buf
        tbl[T_MAIN + 4 * n0 + 1] = pos
        tbl[T_MAIN + 4 * n0 + 2] = r
        tbl[T_MAIN + 4 * n0 + 3] = c
        tbl[T_N0] = n0 + 1

        @pl.when(tile_touch(r, c, 0, 0))
        def _():
            n1 = tbl[T_N1]
            tbl[T_LIST1 + n1] = n0
            tbl[T_N1] = n1 + 1

    def add_send(j, slot):
        for e, side in enumerate((side_near, -side_near)):

            @pl.when(need_s[4 + side, j] == 1)
            def _():
                n = tbl[T_NH + e]
                tbl[T_COL + 12 * e + n] = slot
                tbl[T_NH + e] = n + 1

    def wanted(j, up):
        t = 4 + 3 * up
        return need_s[t - 1, j] | need_s[t, j] | need_s[t + 1, j]

    sent = []
    for up, buf in ((row_near, s_near), (-row_near, s_far)):
        count = jnp.int32(0)
        for s in range(SLOTS):
            flag = wanted(16 + s, up)

            @pl.when(flag == 1)
            def _():
                for p in range(5):
                    buf[count, p] = own[s, p, 0:HALF, :]
                    buf[count + 1, p] = own[s, p, HALF:S, :]

            count = count + 2 * flag
        tbl[T_UNIT] = count

        @pl.loop(0, meta_s[9 + up, 0])
        def _(s):
            r = meta_s[9 + up, 1 + 2 * s] + up * TILE
            c = meta_s[9 + up, 2 + 2 * s]

            @pl.when((r < TILE) & (r + S > 0))
            def _():
                count = tbl[T_UNIT]
                for p in range(4):
                    got = pick(ext, p, r + S, c + HALF, lane_s)
                    buf[count, p] = jnp.where(up == 1, got[0:HALF], got[HALF:S])
                tbl[T_UNIT] = count + 1

        sent.append(tbl[T_UNIT])
    for s in range(SLOTS):

        @pl.when(s < info[0])
        def _():
            add_main(0, s, info[1 + 2 * s], info[2 + 2 * s])
            add_send(16 + s, s)

    got = []
    for up in (-1, 1):
        buf = jnp.where(row_near == up, 0, 1)
        count = jnp.int32(0)
        for s in range(SLOTS):
            j = (4 + 3 * up) * SLOTS + s
            flag = need_s[3, j] | need_s[4, j] | need_s[5, j]

            @pl.when(flag == 1)
            def _():
                r, c, _ = spot(j)
                n = tbl[T_NV]
                tbl[T_CAME + 4 * n] = buf
                tbl[T_CAME + 4 * n + 1] = count
                tbl[T_CAME + 4 * n + 2] = r
                tbl[T_CAME + 4 * n + 3] = c
                tbl[T_NV] = n + 1

                @pl.when(need_s[4, j] == 1)
                def _():
                    add_main(0, SLOTS + n, r, c)

                add_send(j, SLOTS + n)

            count = count + 2 * flag
        for s in range(SLOTS):
            r = info[1 + 2 * s]
            out = (r < 0) if up == -1 else (r + S > TILE)
            there = info[11] + up
            flag = jnp.where((s < info[0]) & out & (there >= 0) & (there < 16), 1, 0)
            tbl[T_PIECE + 2 * s + (up + 1) // 2] = jnp.where(flag == 1, count, -1)
            count = count + flag
        got.append(count)
    got_near = jnp.where(row_near == 1, got[1], got[0])
    got_far = jnp.where(row_near == 1, got[0], got[1])
    for e, (number, most) in enumerate(
        ((b0, jnp.maximum(sent[0], got_near)), (b1, jnp.maximum(sent[1], got_far)))
    ):
        step = step_of(most, ROW_SIZES)
        number[0] = step
        tbl[T_STEP + e] = step

    def ship(act):
        for e, (source, targets) in enumerate(((s_near, to_near), (s_far, to_far))):
            for k, size in enumerate(ROW_SIZES):

                @pl.when(tbl[T_STEP + e] == k + 1)
                def _():
                    act(pltpu.make_async_copy(source.at[0:size], targets[k], sems.at[1 + e]))

    ship(lambda copy: copy.start())

    got = []
    for side in (-1, 1):
        buf = jnp.where(side_near == side, 1, 2)
        count = jnp.int32(0)
        for t in (4 + side, 1 + side, 7 + side):
            for s in range(SLOTS):
                j = t * SLOTS + s
                flag = need_s[4, j]

                @pl.when(flag == 1)
                def _():
                    r, c, _ = spot(j)
                    add_main(buf, count, r, c)

                count = count + flag
        got.append(count)
    got_near = jnp.where(side_near == 1, got[1], got[0])
    got_far = jnp.where(side_near == 1, got[0], got[1])
    step = step_of(jnp.maximum(tbl[T_NH], got_near), CHIP_SIZES)
    tbl[T_STEP + 2] = step
    b2[0] = step
    step = step_of(jnp.maximum(tbl[T_NH + 1], got_far), COL_SIZES)
    tbl[T_STEP + 3] = step
    b3[0] = branch_of(step, tbl[T_NH + 1], got_far, info[9] == 1)
    ship(lambda copy: copy.wait())


def merge(info, tbl, wide, own, *rest):
    rows, chips, cols = len(ROW_SIZES), len(CHIP_SIZES), len(COL_SIZES)
    came = (rest[:rows], rest[rows : 2 * rows])
    out, rest = rest[2 * rows], rest[2 * rows + 1 :]
    targets = (rest[:chips], rest[chips : chips + cols])
    ext, rec, vbuf, sems = rest[chips + cols :]

    def fetch(act):
        for e in range(2):
            for k, size in enumerate(ROW_SIZES):

                @pl.when(tbl[T_STEP + e] == k + 1)
                def _():
                    act(pltpu.make_async_copy(came[e][k], vbuf.at[e, 0:size], sems.at[1 + e]))

    fetch(lambda copy: copy.start())
    copy = pltpu.make_async_copy(wide, ext.at[:, S : S + TILE], sems.at[0])
    copy.start()
    fetch(lambda copy: copy.wait())
    high = lax.broadcasted_iota(I32, (S, S), 0)
    lane = lax.broadcasted_iota(I32, (LONG, S), 1)

    def half(far, unit, p):
        return vbuf[far, unit, p]

    for s in range(SLOTS):

        @pl.when(s < info[0])
        def _():
            for p in range(5):
                rec[s, p] = own[s, p]
            r = info[1 + 2 * s]
            above, below = tbl[T_PIECE + 2 * s], tbl[T_PIECE + 2 * s + 1]
            top = high[0:HALF] + r < 0
            bottom = high[HALF:S] + r >= TILE
            zero = jnp.zeros((HALF, S), F32)

            @pl.when(r < 0)
            def _():
                for p in range(4):
                    part = jnp.where(above >= 0, half(1 - info[10], jnp.maximum(above, 0), p), zero)
                    rec[s, p, 0:HALF] = jnp.where(top, part, rec[s, p, 0:HALF])

            @pl.when(r + S > TILE)
            def _():
                for p in range(4):
                    part = jnp.where(below >= 0, half(info[10], jnp.maximum(below, 0), p), zero)
                    rec[s, p, HALF:S] = jnp.where(bottom, part, rec[s, p, HALF:S])

    copy.wait()

    @pl.loop(0, tbl[T_NV])
    def _(i):
        far = tbl[T_CAME + 4 * i]
        unit = tbl[T_CAME + 4 * i + 1]
        r = tbl[T_CAME + 4 * i + 2]
        c = tbl[T_CAME + 4 * i + 3]
        slot = SLOTS + i
        for p in range(5):
            rec[slot, p, 0:HALF] = half(far, unit, p)
            rec[slot, p, HALF:S] = half(far, unit + 1, p)

        @pl.when((r < TILE) & (r + S > 0))
        def _():
            mine = (high + r >= 0) & (high + r < TILE)
            for p in range(4):
                rec[slot, p] = jnp.where(mine, pick(ext, p, r + S, c + HALF, lane), rec[slot, p])

    many = tbl[T_NV]

    def keep(k):
        return pltpu.make_async_copy(rec.at[k], out.at[k], sems.at[k])

    for e in range(2):

        @pl.loop(0, tbl[T_NH + e])
        def _(i):
            for k, target in enumerate(targets[e]):

                @pl.when(tbl[T_STEP + 2 + e] == k + 1)
                def _():
                    source = rec.at[tbl[T_COL + 12 * e + i]]
                    pltpu.make_async_copy(source, target.at[i], sems.at[12 + 12 * e + i]).start()

    @pl.loop(0, info[0])
    def _(i):
        keep(i).start()

    @pl.loop(SLOTS, SLOTS + many)
    def _(i):
        keep(i).start()

    for e in range(2):

        @pl.loop(0, tbl[T_NH + e])
        def _(i):
            pltpu.make_async_copy(rec.at[0], out.at[0], sems.at[12 + 12 * e + i]).wait()

    @pl.loop(0, info[0])
    def _(i):
        keep(i).wait()

    @pl.loop(SLOTS, SLOTS + many)
    def _(i):
        keep(i).wait()


def times(a, b):
    return (a[0] * b[0] - a[1] * b[1], a[0] * b[1] + a[1] * b[0])


def conj_times(a, b):
    return (a[0] * b[0] + a[1] * b[1], a[0] * b[1] - a[1] * b[0])


def transform(x, left, right):
    return [y for k in range(0, GROUP, 2) for y in transform_pair(x[k : k + 2], left, right)]


def transform_pair(x, left, right):
    half = [jnp.concatenate([w[k].astype(jnp.bfloat16) for w in x], axis=1) for k in range(2)]
    half = jnp.concatenate(half, axis=0)
    half = jnp.dot(left, half, preferred_element_type=F32).astype(jnp.bfloat16)
    half = [jnp.concatenate([half[:S, at], half[S:, at]], axis=1) for at in (slice(0, S), slice(S, 2 * S))]
    done = jnp.dot(jnp.concatenate(half, axis=0), right, preferred_element_type=F32)
    return [(done[at, :S], done[at, S:]) for at in (slice(0, S), slice(S, 2 * S))]


def sweeps(tbl, tile, probe, prop, waves, own, *rest):
    chips, cols = len(CHIP_SIZES), len(COL_SIZES)
    out, rec, acc, sems = rest[chips + cols :]
    sources = [(0, None, own)]
    sources += [(1, k + 1, source) for k, source in enumerate(rest[:chips])]
    sources += [(2, k + 1, source) for k, source in enumerate(rest[chips : chips + cols])]
    n0 = tbl[T_N0]
    n1 = tbl[T_N1]

    @pl.loop(0, n0)
    def _(i):
        buf = tbl[T_MAIN + 4 * i]
        pos = tbl[T_MAIN + 4 * i + 1]
        for b, step, source in sources:

            @pl.when((buf == b) if step is None else ((buf == b) & (tbl[T_STEP + 1 + b] == step)))
            def _():
                pltpu.make_async_copy(source.at[pos], rec.at[i], sems.at[i]).start()

    @pl.loop(0, 12)
    def _(p):
        acc[p, 256:512, 256:512] = jnp.zeros((256, 256), F32)

        @pl.when(p < 6)
        def _():
            acc[p, 128:256, 128:640] = jnp.zeros((128, 512), F32)
            acc[p, 512:640, 128:640] = jnp.zeros((128, 512), F32)
            acc[p, 256:512, 128:256] = jnp.zeros((256, 128), F32)
            acc[p, 256:512, 512:640] = jnp.zeros((256, 128), F32)

    lane = lax.broadcasted_iota(I32, (LONG, S), 1)
    def group(i, base, count, second):
        at = []
        for k in range(GROUP):
            place = GROUP * i + k
            there = place < count
            e = tbl[T_LIST1 + jnp.minimum(place, 35)] if second else place
            e = jnp.where(there, e, 36)
            r = jnp.where(there, tbl[T_MAIN + 4 * e + 2] + TILE, 5 * S)
            c = jnp.where(there, tbl[T_MAIN + 4 * e + 3] + TILE, 0)
            at.append((e, r, c))
            if second:
                high = tbl[T_ROW] + r - TILE + lax.broadcasted_iota(I32, (S, S), 0)
                wide = tbl[T_ROW + 1] + c - TILE + lax.broadcasted_iota(I32, (S, S), 1)
                inside = (high >= 0) & (high < 16 * TILE) & (wide >= 0) & (wide < 16 * TILE)
                for m in range(2):
                    scale = jnp.where(inside, 1.0 / (pick(acc, 4 + m, r, c, lane) + 1.0), 0.0)
                    for p in (2 * m, 2 * m + 1):
                        rec[e, p] = rec[e, p] - pick(acc, p, r, c, lane) * scale
            else:

                @pl.when(there)
                def _():
                    pltpu.make_async_copy(own.at[0], rec.at[e], sems.at[e]).wait()

        wave = (probe[0], probe[1])
        spread = (prop[0], prop[1])
        one, two = waves[0], waves[1]
        exits = [times(wave, (rec[e, 0], rec[e, 1])) for e, _, _ in at]
        inner = transform([times(spread, x) for x in transform(exits, one, two)], two, one)
        o2 = [(rec[e, 2], rec[e, 3]) for e, _, _ in at]
        field = transform([times(x, o) for x, o in zip(inner, o2)], one, two)
        chi = []
        for (e, _, _), f in zip(at, field):
            size = jnp.sqrt(f[0] * f[0] + f[1] * f[1])
            keep = 1.0 - rec[e, 4] / jnp.maximum(size, 1.0)
            chi.append((f[0] * keep, f[1] * keep))
        g2 = transform(chi, two, one)
        for (_, r, c), x, g in zip(at, inner, g2):
            later = conj_times(x, g)
            put(acc, base + 2, r, c, later[0], lane)
            put(acc, base + 3, r, c, later[1], lane)
            put(acc, base + 5, r, c, x[0] * x[0] + x[1] * x[1], lane)
        back = transform([conj_times(o, g) for o, g in zip(o2, g2)], one, two)
        first = transform([conj_times(spread, x) for x in back], two, one)
        light = wave[0] * wave[0] + wave[1] * wave[1]
        for (_, r, c), g in zip(at, first):
            low = conj_times(wave, g)
            put(acc, base, r, c, low[0], lane)
            put(acc, base + 1, r, c, low[1], lane)
            put(acc, base + 4, r, c, light, lane)

    @pl.loop(0, (n0 + GROUP - 1) // GROUP)
    def _(i):
        group(i, 0, n0, False)

    @pl.loop(0, (n1 + GROUP - 1) // GROUP)
    def _(i):
        group(i, 6, n1, True)

    for k in range(2):
        one = 1.0 / (acc[4 + k, 256:512, 256:512] + 1.0)
        two = 1.0 / (acc[10 + k, 256:512, 256:512] + 1.0)
        for p in (2 * k, 2 * k + 1):
            out[p] = tile[p] - acc[p, 256:512, 256:512] * one - acc[6 + p, 256:512, 256:512] * two


VMEM = pl.BlockSpec(memory_space=pltpu.VMEM)
SMEM = pl.BlockSpec(memory_space=pltpu.SMEM)
ANY = pl.BlockSpec(memory_space=pl.ANY)
PARAMS = pltpu.CompilerParams(vmem_limit_bytes=LIMIT)


def shape(*dims, dtype=F32):
    return jax.ShapeDtypeStruct(dims, dtype)


def records(count):
    return shape(count, 5, S, S)


def nothing(out):
    pass


def exchange(sent, branch, axis, ups, downs, kinds):
    def blank(like):
        return pl.pallas_call(nothing, out_shape=shape(*like.shape), out_specs=ANY, name="blank")()

    def of(k, pairs):
        def run(*values):
            got = [blank(value) for value in values]
            if pairs:
                got[k] = lax.ppermute(values[k], axis, pairs)
            return tuple(got)

        return run

    branches = [of(0, None)]
    branches += [of(k, pairs) for k in range(len(sent)) for pairs in (ups + downs, ups, downs)[:kinds]]
    return lax.switch(branch, branches, *sent)


def on_device(object_tiles, probe, prop_phase, amplitudes, offsets, counts):
    row = lax.axis_index("row").astype(I32)
    col = lax.axis_index("col").astype(I32)
    info = jnp.concatenate(
        [counts.reshape(1), offsets.reshape(8), jnp.stack([col % 2, row % 2, row, col]), jnp.zeros((3,), I32)]
    )
    near, far, meta = pl.pallas_call(
        pack_cols,
        out_shape=(shape(512, 128), shape(512, 128), shape(8, 128)),
        in_specs=[SMEM, VMEM],
        out_specs=(VMEM, VMEM, VMEM),
        compiler_params=PARAMS,
        name="pack_cols",
    )(info, object_tiles)
    far = lax.ppermute(far, "col", FAR_UP + FAR_DOWN)
    near = lax.ppermute(near, "col", NEAR_UP + NEAR_DOWN)
    meta_far = lax.ppermute(meta, "row", FAR_UP + FAR_DOWN)
    meta_near = lax.ppermute(meta, "row", NEAR_UP + NEAR_DOWN)
    line = lax.broadcasted_iota(I32, (8, 128), 0)
    odd = row % 2 == 1
    above = jnp.where(odd, meta_near, meta_far)
    below = jnp.where(odd, meta_far, meta_near)
    middle = jnp.where(line == 0, above, jnp.where(line == 1, meta, below))
    meta_far = lax.ppermute(middle, "col", FAR_UP + FAR_DOWN)
    meta_near = lax.ppermute(middle, "col", NEAR_UP + NEAR_DOWN)
    halves = tuple(shape(size, 5, HALF, S) for size in ROW_SIZES)
    rows, chips, cols = len(ROW_SIZES), len(CHIP_SIZES), len(COL_SIZES)
    wide, own, *made = pl.pallas_call(
        plan,
        out_shape=(shape(4, TILE, 384), records(4))
        + halves
        + halves
        + (shape(T_SIZE, dtype=I32),)
        + (shape(1, dtype=I32),) * 4,
        in_specs=[SMEM] + [VMEM] * 7,
        out_specs=(VMEM, VMEM) + (ANY,) * (2 * rows) + (SMEM,) * 5,
        scratch_shapes=[
            pltpu.VMEM((4, 512, 384), F32),
            pltpu.VMEM((12, 5, HALF, S), F32),
            pltpu.VMEM((12, 5, HALF, S), F32),
            pltpu.VMEM((24, 128), I32),
            pltpu.SMEM((24, 128), I32),
            pltpu.SMEM((16, 128), I32),
            pltpu.SemaphoreType.DMA((3,)),
        ],
        compiler_params=PARAMS,
        name="plan",
    )(info, object_tiles, near, far, middle, meta_near, meta_far, amplitudes)
    tbl, b0, b1, b2, b3 = made[2 * rows :]
    v_far = exchange(made[rows : 2 * rows], b1[0], "row", FAR_UP, FAR_DOWN, 1)
    v_near = exchange(made[:rows], b0[0], "row", NEAR_UP, NEAR_DOWN, 1)
    own, *made = pl.pallas_call(
        merge,
        out_shape=(records(12),) + tuple(records(size) for size in CHIP_SIZES + COL_SIZES),
        in_specs=[SMEM, SMEM, ANY, VMEM] + [ANY] * (2 * rows),
        out_specs=(ANY,) * (1 + chips + cols),
        scratch_shapes=[
            pltpu.VMEM((4, 512, 384), F32),
            pltpu.VMEM((12, 5, S, S), F32),
            pltpu.VMEM((2, 12, 5, HALF, S), F32),
            pltpu.SemaphoreType.DMA((36,)),
        ],
        compiler_params=PARAMS,
        name="merge",
    )(info, tbl, wide, own, *v_near, *v_far)
    h_far = exchange(made[chips:], b3[0], "col", FAR_UP, FAR_DOWN, 3)
    h_near = exchange(made[:chips], b2[0], "col", NEAR_UP, NEAR_DOWN, 1)
    prop = jnp.stack([jnp.cos(prop_phase), jnp.sin(prop_phase)])
    return pl.pallas_call(
        sweeps,
        out_shape=shape(4, TILE, TILE),
        in_specs=[SMEM, VMEM, VMEM, VMEM, VMEM] + [ANY] * (1 + chips + cols),
        out_specs=VMEM,
        scratch_shapes=[
            pltpu.VMEM((37, 5, S, S), F32),
            pltpu.VMEM((12, 776, 768), F32),
            pltpu.SemaphoreType.DMA((36,)),
        ],
        compiler_params=PARAMS,
        name="sweeps",
    )(tbl, object_tiles, probe, prop, jnp.asarray(wave_tables()), own, *h_near, *h_far)


def solution(mesh):
    return jax.shard_map(
        on_device,
        mesh=mesh,
        in_specs=(
            P(None, "row", "col"),
            P(),
            P(),
            P(None, "row", "col"),
            P("row", "col", None, None),
            P("row", "col"),
        ),
        out_specs=P(None, "row", "col"),
        check_vma=False,
    )
```
